512 devices in a mesh: seq: 128 (over x, y, z_lo, core), head: 4 (over z_hi).
Axes of the slice: x: 4, y: 4, z: 16 (z_hi: 4, z_lo: 4; z = z_hi * 4 + z_lo), core: 2. Of those that a mesh axis runs over, the one named last changes fastest.
Arguments:
- queries: bfloat16 [16, 32768, 128], P('head', 'seq'), may hold values from -9 to 9
- key_vectors: bfloat16 [16, 32768, 128], P('head', 'seq'), may hold values from -9 to 9
- value_vectors: bfloat16 [16, 32768, 128], P('head', 'seq'), may hold values from -16 to 16
- block_perm: int32 [16, 64], P('head'), may hold values from 0 to 63, each once within a row
- out_weight: bfloat16 [16, 128, 2048], P('head'), may hold values from -0.125 to 0.125
- out_cotangent: bfloat16 [32768, 2048], P('seq', 'head'), may hold values from -6 to 6
Outputs:
- projected: bfloat16 [32768, 2048], P('seq', 'head')
- gradient_of_queries: bfloat16 [16, 32768, 128], P('head', 'seq')
- key_grad: bfloat16 [16, 32768, 128], P('head', 'seq')
- value_grad: bfloat16 [16, 32768, 128], P('head', 'seq')
The draws below stay inside these ranges and needn't reach their ends.
Inputs may be any that keep to these rules, and one draw needn't show every extreme that they name: Each row of block_perm names every block of 0 to 63 once.
All inputs are finite; a program needn't handle non-finite values.
Results may differ from the reference program's by a relative error of at most 0.029.
Values may be sent and summed in bfloat16 or wider, within the bound.
A program may use at most 64 MiB of HBM per device.

```python
import math
from functools import partial
import jax
import jax.numpy as jnp
from jax import lax

HD = 128
HEADS = 16
DOUT = 2048
BLOCK = 512
TOK_DEV = 256
TOKENS = 32768
NBLK = 64


def paired_rows(key):
    base = jax.random.fold_in(key, 7)
    first_key, second_key = jax.random.split(base, 2)
    shape = (HEADS, TOKENS, HD)
    query_part = jnp.clip(1.2 * jax.random.normal(first_key, shape, jnp.float32), -5.0, 5.0)
    key_part = jnp.clip(1.2 * jax.random.normal(second_key, shape, jnp.float32), -5.0, 5.0)
    return (query_part, key_part)


def draw_queries(key, part):
    return paired_rows(key)[0].astype(jnp.bfloat16)


def draw_key_vectors(key, part):
    return paired_rows(key)[1].astype(jnp.bfloat16)


def levels(stream_key, dims, pieces, smallest, top_value):
    level, own = 1.0, jax.random.fold_in(stream_key, 6)
    for axis_at, shards_of in pieces:
        steps = jnp.exp(jax.random.uniform(jax.random.fold_in(own, axis_at), (shards_of,), jnp.float32, smallest / len(pieces), top_value / len(pieces)))
        level = level * jnp.repeat(steps, dims[axis_at] // shards_of).reshape([-1 if axis == axis_at else 1 for axis in range(len(dims))])
    return level


def scatter_about(key, extent, deviation, most, pieces=(), held_as=jnp.bfloat16):
    loudness = levels(key, extent, pieces, -0.22, 0.18) if pieces else 1.0
    result = jax.random.normal(key, extent, jnp.float32) * deviation * loudness
    return jnp.minimum(jnp.maximum(result, -most), most).astype(held_as)


def setup_inputs(seed: int = 0) -> dict:
    splits = jax.random.split(jax.random.key(seed), 7)
    queries = draw_queries(jax.random.fold_in(splits[6], 71), 0)
    key_vectors = draw_key_vectors(jax.random.fold_in(splits[6], 71), 0)
    value_vectors = scatter_about(splits[2], (HEADS, TOKENS, HD), 4.0, 16.0, ((0, 4), (1, 128)))
    block_perm = jax.vmap(lambda own: jax.random.permutation(own, NBLK))(jax.random.split(splits[3], HEADS)).reshape((HEADS, NBLK)).astype(jnp.int32)
    out_weight = scatter_about(splits[4], (HEADS, HD, DOUT), (HEADS * HD) ** -0.5, 0.125, ((0, 4),))
    out_cotangent = scatter_about(splits[5], (TOKENS, DOUT), 1.0, 6.0, ((0, 128), (1, 4)))
    return {"queries": queries, "key_vectors": key_vectors, "value_vectors": value_vectors, "block_perm": block_perm, "out_weight": out_weight, "out_cotangent": out_cotangent}


def to_low(values):
    return lax.optimization_barrier(values.astype(jnp.bfloat16)).astype(jnp.float32)

def split_terms(half_terms, order, nblocks):
    local = half_terms[:, :, :BLOCK].reshape(nblocks, 2, 2, TOK_DEV, HD)
    own = jnp.stack([local[:, 0, 0], local[:, 1, 1]], axis=1).reshape(nblocks, BLOCK, HD)
    pair = jnp.stack([local[:, 1, 0], local[:, 0, 1]], axis=1).reshape(nblocks, BLOCK, HD)
    partner = to_low(half_terms[:, 0, BLOCK:]) + to_low(half_terms[:, 1, BLOCK:])
    zeros_blocks = jnp.zeros((nblocks, BLOCK, HD), jnp.float32)
    moved = zeros_blocks.at[order].add(partner)
    remote = to_low(to_low(pair) + moved)
    return (own + remote).astype(jnp.bfloat16).reshape(TOKENS, HD)

def head_pass(cotangent, carry, inputs):
    query_rows, key_rows, value_rows, order, weight_rows = inputs
    nblocks = TOKENS // BLOCK
    scale_factor = 1.0 / math.sqrt(HD)
    query_by_block = query_rows.reshape(nblocks, BLOCK, HD).astype(jnp.float32)
    blocked_k = key_rows.reshape(nblocks, BLOCK, HD).astype(jnp.float32)
    blocked_v = value_rows.reshape(nblocks, BLOCK, HD).astype(jnp.float32)
    joined_keys = jnp.concatenate([blocked_k, blocked_k[order]], axis=1)
    joined_values = jnp.concatenate([blocked_v, blocked_v[order]], axis=1)
    logit_scores = jnp.einsum('nsx,nox->nso', query_by_block, joined_keys) * scale_factor
    row_max = lax.optimization_barrier(jnp.max(logit_scores, axis=-1, keepdims=True))
    weights = jnp.exp(logit_scores - row_max)
    probabilities = weights / lax.optimization_barrier(jnp.sum(weights, axis=-1, keepdims=True))
    reduced_probabilities = lax.optimization_barrier(probabilities.astype(jnp.bfloat16)).astype(jnp.float32)
    attention_result = jnp.einsum('osa,oam->osm', reduced_probabilities, joined_values).astype(jnp.bfloat16)
    attention_result = lax.optimization_barrier(attention_result)
    flat_att = attention_result.reshape(TOKENS, HD)
    carry = carry + jnp.dot(flat_att, weight_rows, preferred_element_type=jnp.float32)
    grad_att = jnp.dot(cotangent, weight_rows.T, preferred_element_type=jnp.float32).astype(jnp.bfloat16)
    grad_att = lax.optimization_barrier(grad_att)
    gradient_by_block = grad_att.reshape(nblocks, BLOCK, HD).astype(jnp.float32)
    row_delta = lax.optimization_barrier(jnp.sum(gradient_by_block * attention_result.astype(jnp.float32), axis=-1, keepdims=True))
    probability_gradient = jnp.einsum('nsx,nox->nso', gradient_by_block, joined_values)
    score_gradient = (probabilities * (probability_gradient - row_delta) * scale_factor).astype(jnp.bfloat16)
    score_gradient = lax.optimization_barrier(score_gradient).astype(jnp.float32)
    gradient_of_queries = jnp.einsum('osa,oam->osm', score_gradient, joined_keys).astype(jnp.bfloat16)
    halves_s = score_gradient.reshape(nblocks, 2, TOK_DEV, 2 * BLOCK)
    halves_p = reduced_probabilities.reshape(nblocks, 2, TOK_DEV, 2 * BLOCK)
    halves_q = query_by_block.reshape(nblocks, 2, TOK_DEV, HD)
    halves_g = gradient_by_block.reshape(nblocks, 2, TOK_DEV, HD)
    key_half = jnp.einsum('burk,burd->bukd', halves_s, halves_q)
    value_half = jnp.einsum('burk,burd->bukd', halves_p, halves_g)
    outputs = (gradient_of_queries.reshape(TOKENS, HD), split_terms(key_half, order, nblocks), split_terms(value_half, order, nblocks))
    return (carry, outputs)

def reference(queries, key_vectors, value_vectors, block_perm, out_weight, out_cotangent):
    initial = jnp.zeros((TOKENS, DOUT), jnp.float32)
    summed, grads = lax.scan(partial(head_pass, out_cotangent), initial, (queries, key_vectors, value_vectors, block_perm, out_weight))
    return (summed.astype(jnp.bfloat16), grads[0], grads[1], grads[2])
```

```python
import functools
import math

import jax
import jax.numpy as jnp
from jax import lax
from jax.experimental import pallas as pl
from jax.experimental.pallas import tpu as pltpu
from jax.sharding import PartitionSpec as P

MESH = pl.DeviceIdType.MESH
BF = jnp.bfloat16
F32 = jnp.float32


def nn(a, b):
    return lax.dot_general(a, b, (((1,), (0,)), ((), ())), preferred_element_type=F32)


def nt(a, b):
    return lax.dot_general(a, b, (((1,), (1,)), ((), ())), preferred_element_type=F32)


def tn(a, b):
    return lax.dot_general(a, b, (((0,), (0,)), ((), ())), preferred_element_type=F32)


def peer_chip(me, step, chips):
    if chips != 64:
        return lax.rem(me + step, chips)
    out = 0
    for unit in (16, 4, 1):
        digit = lax.rem(lax.div(me, unit), 4) + lax.rem(lax.div(step, unit), 4)
        out = out + unit * lax.rem(digit, 4)
    return out


def kernel(
    dims,
    perm_ref, inv_ref, q_hbm, k_hbm, v_hbm, w_hbm, cot_hbm,
    proj_ref, dq_ref, dk_ref, dv_ref,
    kv, q, w, cot, in1, out1, in3, out3, back, prob, att, grad, att_t, grad_t,
    own, give, got, part, rs_far, rs_near,
    load_sem, a2a_send, a2a_recv, pair_send, pair_recv, ag_send, ag_recv, rs_send, rs_recv,
):
    heads, tok, width, chips, groups = dims
    seq = lax.axis_index("seq")
    hi = lax.axis_index("head")
    core = lax.rem(seq, 2)
    me = lax.div(seq, 2)
    sibling = {"seq": me * 2 + 1 - core}
    up, down = lax.rem(hi + 1, groups), lax.rem(hi + groups - 1, groups)
    far = lax.rem(hi + 2, groups)
    to_up, to_down = {"head": up}, {"head": down}
    per_head = chips // (2 * heads)
    mid = tok // 2
    my_head = lax.rem(lax.div(me, per_head), heads)
    scale = 1.0 / math.sqrt(width)

    def on_chip(p):
        return {"seq": p * 2 + core}

    def remote(src, dst, send, recv, where):
        return pltpu.make_async_remote_copy(
            src_ref=src, dst_ref=dst, send_sem=send, recv_sem=recv,
            device_id=where, device_id_type=MESH,
        )

    def arrived(ref, sem):
        pltpu.make_async_copy(ref, ref, sem).wait()

    half = chips // 2
    load_k = pltpu.make_async_copy(k_hbm, kv.at[0, pl.ds(0, half)], load_sem.at[0])
    load_v = pltpu.make_async_copy(v_hbm, kv.at[0, pl.ds(half, half)], load_sem.at[1])
    load_cot = pltpu.make_async_copy(cot_hbm, cot.at[hi], load_sem.at[2])
    load_q = pltpu.make_async_copy(q_hbm, q, load_sem.at[3])
    cols = cot_hbm.shape[1]
    load_w = [
        pltpu.make_async_copy(w_hbm.at[:, pl.ds(c * cols, cols)], w.at[c], load_sem.at[4 + c])
        for c in range(groups)
    ]
    for copy in [load_k, load_v, load_cot, load_q] + load_w:
        copy.start()

    barrier = pltpu.get_barrier_semaphore()

    def greet(step, carry):
        pl.semaphore_signal(
            barrier, inc=1, device_id=on_chip(peer_chip(me, step, chips)), device_id_type=MESH
        )
        return carry

    lax.fori_loop(1, chips, greet, 0)
    for where in (sibling, to_up, to_down):
        pl.semaphore_signal(barrier, inc=1, device_id=where, device_id_type=MESH)
    load_k.wait()
    load_v.wait()
    pl.semaphore_wait(barrier, chips - 1 + 3)

    def spread(src, dst, phase):
        def body(step, carry):
            p = peer_chip(me, step, chips)
            remote(src.at[p], dst.at[me], a2a_send.at[phase], a2a_recv.at[phase], on_chip(p)).start()
            return carry

        lax.fori_loop(1, chips, body, 0)
        dst[me] = src[me]

    def forward(src, table, out, dst, phase):
        def body(step, carry):
            p = peer_chip(me, step, chips)
            out[p] = src[table[my_head, p]]
            remote(out.at[p], dst.at[me], a2a_send.at[phase], a2a_recv.at[phase], on_chip(p)).start()
            return carry

        lax.fori_loop(1, chips, body, 0)
        dst[me] = src[table[my_head, me]]

    def all_arrived(dst, phase):
        arrived(dst.at[pl.ds(0, chips - 1)], a2a_recv.at[phase])

    spread(kv.at[0], in1, 0)
    swap_own = remote(kv.at[0], kv.at[1], pair_send.at[0], pair_recv.at[0], sibling)
    swap_own.start()

    load_cot.wait()
    lo, top = pl.ds(0, mid), pl.ds(mid, mid)
    ag_up = [
        remote(cot.at[hi, s], cot.at[hi, s], ag_send.at[i], ag_recv.at[i], to_up)
        for i, s in enumerate((lo, top))
    ]
    ag_down = [
        remote(cot.at[hi, s], cot.at[hi, s], ag_send.at[2 + i], ag_recv.at[2 + i], to_down)
        for i, s in enumerate((top, lo))
    ]
    for copy in (ag_up[0], ag_down[0], ag_up[1], ag_down[1]):
        copy.start()

    all_arrived(in1, 0)
    forward(in1, perm_ref, out1, kv.at[2], 1)

    ag_up[0].wait_recv()
    pass_up = remote(cot.at[down, lo], cot.at[down, lo], ag_send.at[4], ag_recv.at[4], to_up)
    pass_up.start()
    ag_down[0].wait_recv()
    pass_down = remote(cot.at[up, top], cot.at[up, top], ag_send.at[5], ag_recv.at[5], to_down)
    pass_down.start()

    load_q.wait()
    all_arrived(kv.at[2], 1)
    swap_partner = remote(kv.at[2], kv.at[3], pair_send.at[1], pair_recv.at[1], sibling)
    swap_partner.start()
    swap_own.wait_recv()
    swap_partner.wait_recv()

    def rows_of(slot, which, h):
        piece = kv[slot, pl.ds((which * heads + h) * per_head, per_head)]
        return piece.reshape(tok, width)

    def attend(h, carry):
        q_h = q[h]
        scores = [nt(rows_of(slot, 0, h), q_h) for slot in range(4)]
        top_score = functools.reduce(
            jnp.maximum, [jnp.max(s, axis=0, keepdims=True) for s in scores]
        )
        weights = [jnp.exp2((s - top_score) * (scale * math.log2(math.e))) for s in scores]
        total = functools.reduce(
            jnp.add, [jnp.sum(e, axis=0, keepdims=True) for e in weights]
        )
        inverse = 1.0 / total
        acc = None
        for slot in range(4):
            low = (weights[slot] * inverse).astype(BF)
            prob[h, slot] = low
            term = tn(rows_of(slot, 1, h), low)
            acc = term if acc is None else acc + term
        low = acc.astype(BF)
        att_t[h] = low
        att[h] = low.T
        return carry

    lax.fori_loop(0, heads, attend, 0)

    for copy in load_w:
        copy.wait()

    def project(c):
        acc = None
        for h in range(heads):
            term = nn(att[h], w[c, pl.ds(h * width, width)])
            acc = term if acc is None else acc + term
        part[c] = acc.astype(BF)

    project(far)
    rs_a = remote(part.at[far, lo], rs_far.at[0], rs_send.at[0], rs_recv.at[0], to_up)
    rs_b = remote(part.at[far, top], rs_far.at[1], rs_send.at[1], rs_recv.at[1], to_down)
    rs_a.start()
    rs_b.start()
    project(up)
    rs_c = remote(part.at[up, top], rs_near.at[0, top], rs_send.at[2], rs_recv.at[2], to_up)
    rs_c.start()
    project(down)
    rs_d = remote(part.at[down, lo], rs_near.at[1, lo], rs_send.at[3], rs_recv.at[3], to_down)
    rs_d.start()
    project(hi)

    ag_up[1].wait_recv()
    ag_down[1].wait_recv()
    pass_up.wait_recv()
    pass_down.wait_recv()

    def pull(h, carry):
        acc = None
        for c in range(groups):
            term = nt(cot[c], w[c, pl.ds(pl.multiple_of(h * width, width), width)])
            acc = term if acc is None else acc + term
        low = acc.astype(BF)
        grad[h] = low
        grad_t[h] = low.T
        return carry

    lax.fori_loop(0, heads, pull, 0)

    def differentiate(h, carry):
        q_h = q[h]
        grad_h = grad[h]
        delta = jnp.sum(
            grad_t[h].astype(F32) * att_t[h].astype(F32), axis=0, keepdims=True
        )
        dq_t = None
        for slot in range(4):
            low = prob[h, slot]
            d_prob = nt(rows_of(slot, 1, h), grad_h)
            d_score = (low.astype(F32) * ((d_prob - delta) * scale)).astype(BF)
            term = tn(rows_of(slot, 0, h), d_score)
            dq_t = term if dq_t is None else dq_t + term
            d_key = nn(d_score, q_h)
            d_value = nn(low, grad_h)
            for which, value in ((0, d_key), (1, d_value)):
                value = value.reshape(per_head, tok // per_head, width)
                where = pl.ds((which * heads + h) * per_head, per_head)
                if slot == 0:
                    own[where] = value
                else:
                    give[slot - 1, where] = value.astype(BF)
        dq_ref[h] = dq_t.T.astype(BF)
        return carry

    lax.fori_loop(0, heads, differentiate, 0)

    swap_pair = remote(give.at[0], got.at[0], pair_send.at[2], pair_recv.at[2], sibling)
    swap_term = remote(give.at[2], got.at[1], pair_send.at[3], pair_recv.at[3], sibling)
    swap_term.start()
    swap_pair.start()
    swap_term.wait_recv()
    both = give[1].astype(F32) + got[1].astype(F32)
    give[1] = both.astype(BF)

    spread(give.at[1], in3, 2)

    rs_a.wait_recv()
    part[up, lo] = (part[up, lo].astype(F32) + rs_far[0].astype(F32)).astype(BF)
    rs_e = remote(part.at[up, lo], rs_near.at[0, lo], rs_send.at[4], rs_recv.at[4], to_up)
    rs_e.start()
    rs_b.wait_recv()
    part[down, top] = (part[down, top].astype(F32) + rs_far[1].astype(F32)).astype(BF)
    rs_f = remote(part.at[down, top], rs_near.at[1, top], rs_send.at[5], rs_recv.at[5], to_down)
    rs_f.start()

    all_arrived(in3, 2)
    forward(in3, inv_ref, out3, back, 3)

    swap_pair.wait_recv()
    for copy in (rs_c, rs_d, rs_e, rs_f):
        copy.wait_recv()
    proj_ref[...] = (
        part[hi].astype(F32) + rs_near[0].astype(F32) + rs_near[1].astype(F32)
    ).astype(BF)

    all_arrived(back, 3)

    def finish(h, carry):
        for which, ref in ((0, dk_ref), (1, dv_ref)):
            where = pl.ds((which * heads + h) * per_head, per_head)
            remote_sum = (back[where].astype(F32) + got[0, where].astype(F32)).astype(BF)
            total = own[where] + remote_sum.astype(F32)
            ref[h] = total.astype(BF).reshape(tok, width)
        return carry

    lax.fori_loop(0, heads, finish, 0)

    for phase, ref in enumerate((kv.at[0], out1, give.at[1], out3)):
        arrived(ref.at[pl.ds(0, chips - 1)], a2a_send.at[phase])
    for copy in (
        [swap_own, swap_partner, swap_pair, swap_term, pass_up, pass_down]
        + ag_up + ag_down + [rs_a, rs_b, rs_c, rs_d, rs_e, rs_f]
    ):
        copy.wait_send()


def per_device(queries, key_vectors, value_vectors, block_perm, out_weight, out_cotangent):
    chips = lax.axis_size("seq") // 2
    groups = lax.axis_size("head")
    heads, tok, width = queries.shape
    rows = 2 * heads * tok // chips
    cols = out_cotangent.shape[1]
    blocks = lax.iota(jnp.int32, chips)
    inverse = jnp.sum(
        jnp.where(block_perm[:, None, :] == blocks[None, :, None], blocks[None, None, :], 0), axis=2
    )
    any_space = pl.BlockSpec(memory_space=pl.ANY)
    smem = pl.BlockSpec(memory_space=pltpu.SMEM)
    vmem = pl.BlockSpec(memory_space=pltpu.VMEM)
    mat = jax.ShapeDtypeStruct((heads, tok, width), BF)
    pieces = (chips, rows, width)
    dma = pltpu.SemaphoreType.DMA
    scratch = [
        pltpu.VMEM((4,) + pieces, BF),
        pltpu.VMEM((heads, tok, width), BF),
        pltpu.VMEM((groups, heads * width, cols), BF),
        pltpu.VMEM((groups, tok, cols), BF),
        pltpu.VMEM(pieces, BF),
        pltpu.VMEM(pieces, BF),
        pltpu.VMEM(pieces, BF),
        pltpu.VMEM(pieces, BF),
        pltpu.VMEM(pieces, BF),
        pltpu.VMEM((heads, 4, tok, tok), BF),
        pltpu.VMEM((heads, tok, width), BF),
        pltpu.VMEM((heads, tok, width), BF),
        pltpu.VMEM((heads, width, tok), BF),
        pltpu.VMEM((heads, width, tok), BF),
        pltpu.VMEM(pieces, F32),
        pltpu.VMEM((3,) + pieces, BF),
        pltpu.VMEM((2,) + pieces, BF),
        pltpu.VMEM((groups, tok, cols), BF),
        pltpu.VMEM((2, tok // 2, cols), BF),
        pltpu.VMEM((2, tok, cols), BF),
        dma((8,)), dma((4,)), dma((4,)), dma((4,)), dma((4,)), dma((6,)), dma((6,)), dma((6,)), dma((6,)),
    ]
    return pl.pallas_call(
        functools.partial(kernel, (heads, tok, width, chips, groups)),
        out_shape=(jax.ShapeDtypeStruct((tok, cols), BF), mat, mat, mat),
        in_specs=[smem, smem] + [any_space] * 5,
        out_specs=(vmem,) * 4,
        scratch_shapes=scratch,
        compiler_params=pltpu.CompilerParams(
            collective_id=0, has_side_effects=True, vmem_limit_bytes=48 << 20
        ),
    )(
        block_perm,
        inverse,
        queries,
        key_vectors.reshape(chips // 2, rows, width),
        value_vectors.reshape(chips // 2, rows, width),
        out_weight.reshape(heads * width, -1),
        out_cotangent,
    )


def solution(mesh):
    return jax.shard_map(
        per_device,
        mesh=mesh,
        in_specs=(
            P("head", "seq", None),
            P("head", "seq", None),
            P("head", "seq", None),
            P("head", None),
            P("head", None, None),
            P("seq", "head"),
        ),
        out_specs=(
            P("seq", "head"),
            P("head", "seq", None),
            P("head", "seq", None),
            P("head", "seq", None),
        ),
        check_vma=False,
    )
```

```python
import functools
import math

import jax
import jax.numpy as jnp
from jax import lax
from jax.experimental import pallas as pl
from jax.experimental.pallas import tpu as pltpu
from jax.sharding import PartitionSpec as P

MESH = pl.DeviceIdType.MESH
BF = jnp.bfloat16
F32 = jnp.float32


def nn(a, b):
    return lax.dot_general(a, b, (((1,), (0,)), ((), ())), preferred_element_type=F32)


def nt(a, b):
    return lax.dot_general(a, b, (((1,), (1,)), ((), ())), preferred_element_type=F32)


def tn(a, b):
    return lax.dot_general(a, b, (((0,), (0,)), ((), ())), preferred_element_type=F32)


def digits(chips):
    side = round(chips ** (1 / 3))
    return (side * side, side, 1), side


def peer_chip(me, step, chips):
    units, side = digits(chips)
    out = 0
    for unit in units:
        digit = lax.rem(lax.div(me, unit), side) + lax.rem(lax.div(step, unit), side)
        out = out + unit * lax.rem(digit, side)
    return out


def kernel(
    dims,
    perm_ref, inv_ref, q_hbm, k_hbm, v_hbm, w_hbm, cot_hbm,
    proj_ref, dq_ref, dk_ref, dv_ref,
    kv, q, w, wx, cot, cot_m, gp_out, gp_in, g_acc,
    in1, out1, in3, out3, back, prob, att, att_m, att_t, grad, pp_out, pp_in,
    own, give, got,
    load_sem, a2a_send, a2a_recv, pair_send, pair_recv, wx_send, wx_recv, hd_send, hd_recv,
):
    heads, tok, width, chips, groups = dims
    seq = lax.axis_index("seq")
    hi = lax.axis_index("head")
    core = lax.rem(seq, 2)
    me = lax.div(seq, 2)
    sibling = {"seq": me * 2 + 1 - core}
    near = (hi + 1 - 2 * lax.rem(hi, 2), groups - 1 - hi)
    per_head = chips // (2 * heads)
    mid = tok // 2
    side_rows = (pl.ds(0, mid), pl.ds(mid, mid))
    my_head = lax.rem(lax.div(me, per_head), heads)
    scale = 1.0 / math.sqrt(width)

    def on_chip(p):
        return {"seq": p * 2 + core}

    def remote(src, dst, send, recv, where):
        return pltpu.make_async_remote_copy(
            src_ref=src, dst_ref=dst, send_sem=send, recv_sem=recv,
            device_id=where, device_id_type=MESH,
        )

    def arrived(ref, sem):
        pltpu.make_async_copy(ref, ref, sem).wait()

    half = chips // 2
    load_k = pltpu.make_async_copy(k_hbm, kv.at[0, pl.ds(0, half)], load_sem.at[0])
    load_v = pltpu.make_async_copy(v_hbm, kv.at[0, pl.ds(half, half)], load_sem.at[1])
    load_cot = pltpu.make_async_copy(cot_hbm, cot, load_sem.at[2])
    load_q = pltpu.make_async_copy(q_hbm, q, load_sem.at[3])
    cols = cot_hbm.shape[1]
    load_w = [
        pltpu.make_async_copy(w_hbm.at[:, pl.ds(c * cols, cols)], w.at[c], load_sem.at[4 + c])
        for c in range(groups)
    ]
    for copy in [load_k, load_v] + load_w + [load_cot, load_q]:
        copy.start()

    barrier = pltpu.get_barrier_semaphore()

    def greet(step, carry):
        pl.semaphore_signal(
            barrier, inc=1, device_id=on_chip(peer_chip(me, step, chips)), device_id_type=MESH
        )
        return carry

    lax.fori_loop(1, chips, greet, 0)
    for where in (sibling, {"head": near[0]}, {"head": near[1]}):
        pl.semaphore_signal(barrier, inc=1, device_id=where, device_id_type=MESH)
    for copy in [load_k, load_v] + load_w + [load_cot, load_q]:
        copy.wait()
    pl.semaphore_wait(barrier, chips - 1 + 3)

    wx_rows = wx.shape[2]
    blocks = chips // 2
    giver = near[0] + core * (near[1] - near[0])
    opposite = groups - 1 - near[0]
    block = lax.div(me, blocks)
    column = giver + block * (opposite - giver)
    row = pl.ds(pl.multiple_of(lax.rem(me, blocks) * wx_rows, wx_rows), wx_rows)
    wx_cross = remote(
        w.at[column, row], wx.at[core, me], wx_send.at[0], wx_recv.at[0], {"head": giver}
    )
    wx_cross.start()
    units, side = digits(chips)

    def wx_stage(axis):
        unit = units[axis]
        digit = lax.rem(lax.div(me, unit), side)
        have = wx.at[core, pl.ds(lax.div(me, unit) * unit, unit)]
        for j in range(1, side):
            p = me + (lax.rem(digit + j, side) - digit) * unit
            remote(have, have, wx_send.at[1 + axis], wx_recv.at[1 + axis], on_chip(p)).start()

    def wx_stage_span(axis):
        return wx.at[core, pl.ds(0, (side - 1) * units[axis])]

    def spread(src, dst, phase):
        def body(step, carry):
            p = peer_chip(me, step, chips)
            remote(src.at[p], dst.at[me], a2a_send.at[phase], a2a_recv.at[phase], on_chip(p)).start()
            return carry

        lax.fori_loop(1, chips, body, 0)
        dst[me] = src[me]

    def forward(src, table, out, dst, phase):
        def body(step, carry):
            p = peer_chip(me, step, chips)
            out[p] = src[table[my_head, p]]
            remote(out.at[p], dst.at[me], a2a_send.at[phase], a2a_recv.at[phase], on_chip(p)).start()
            return carry

        lax.fori_loop(1, chips, body, 0)
        dst[me] = src[table[my_head, me]]

    def all_arrived(dst, phase):
        arrived(dst.at[pl.ds(0, chips - 1)], a2a_recv.at[phase])

    def to_near(src, dst, slot, side):
        return remote(src, dst, hd_send.at[slot], hd_recv.at[slot], {"head": near[side]})

    spread(kv.at[0], in1, 0)
    swap_own = remote(kv.at[0], kv.at[1], pair_send.at[0], pair_recv.at[0], sibling)
    swap_own.start()
    cot_swap = [to_near(cot.at[side_rows[t]], cot_m.at[t], t, t) for t in range(2)]
    for copy in cot_swap:
        copy.start()

    wx_cross.wait_recv()
    wx_stage(2)
    arrived(wx_stage_span(2), wx_recv.at[3])
    wx_stage(1)
    all_arrived(in1, 0)
    forward(in1, perm_ref, out1, kv.at[2], 1)
    arrived(wx_stage_span(1), wx_recv.at[2])
    wx_stage(0)

    def neighbour_w(source, which):
        return wx[source, pl.ds(which * blocks, blocks)].reshape(blocks * wx_rows, cols)

    for t in range(2):
        cot_swap[t].wait_recv()
        g_acc[t] = nt(cot[side_rows[t]], w[hi]) + nt(cot_m[t], w[near[t]])

    arrived(wx_stage_span(0), wx_recv.at[1])
    swap_wx = remote(wx.at[core], wx.at[core], pair_send.at[4], pair_recv.at[4], sibling)
    swap_wx.start()
    swap_wx.wait_recv()
    gp_swap = []
    for t in range(2):
        both = nt(cot[side_rows[t]], neighbour_w(1 - t, 0)) + nt(cot_m[t], neighbour_w(1 - t, 1))
        gp_out[t] = both.astype(BF)
        gp_swap.append(to_near(gp_out.at[t], gp_in.at[t], 2 + t, 1 - t))
        gp_swap[t].start()

    all_arrived(kv.at[2], 1)
    swap_partner = remote(kv.at[2], kv.at[3], pair_send.at[1], pair_recv.at[1], sibling)
    swap_partner.start()
    swap_own.wait_recv()
    swap_partner.wait_recv()

    def rows_of(slot, which, h):
        piece = kv[slot, pl.ds((which * heads + h) * per_head, per_head)]
        return piece.reshape(tok, width)

    def attend(h, carry):
        q_h = q[h]
        scores = [nt(rows_of(slot, 0, h), q_h) for slot in range(4)]
        top_score = functools.reduce(
            jnp.maximum, [jnp.max(s, axis=0, keepdims=True) for s in scores]
        )
        weights = [jnp.exp2((s - top_score) * (scale * math.log2(math.e))) for s in scores]
        total = functools.reduce(
            jnp.add, [jnp.sum(e, axis=0, keepdims=True) for e in weights]
        )
        inverse = 1.0 / total
        acc = None
        for slot in range(4):
            low = (weights[slot] * inverse).astype(BF)
            prob[h, slot] = low
            term = tn(rows_of(slot, 1, h), low)
            acc = term if acc is None else acc + term
        low = acc.astype(BF)
        att_t[h] = low
        att[:, pl.ds(pl.multiple_of(h * width, width), width)] = low.T
        return carry

    lax.fori_loop(0, heads, attend, 0)

    att_swap = [to_near(att.at[side_rows[t]], att_m.at[t], 4 + t, t) for t in range(2)]
    for copy in att_swap:
        copy.start()

    for t in range(2):
        gp_swap[t].wait_recv()
        both = (g_acc[t] + gp_in[t].astype(F32)).astype(BF)
        for h in range(heads):
            grad[h, side_rows[t]] = both[:, h * width:(h + 1) * width]

    def differentiate(h, carry):
        q_h = q[h]
        grad_h = grad[h]
        delta = jnp.sum(
            grad_h.T.astype(F32) * att_t[h].astype(F32), axis=0, keepdims=True
        )
        dq_t = None
        for slot in range(4):
            low = prob[h, slot]
            d_prob = nt(rows_of(slot, 1, h), grad_h)
            d_score = (low.astype(F32) * ((d_prob - delta) * scale)).astype(BF)
            term = tn(rows_of(slot, 0, h), d_score)
            dq_t = term if dq_t is None else dq_t + term
            d_key = nn(d_score, q_h)
            d_value = nn(low, grad_h)
            for which, value in ((0, d_key), (1, d_value)):
                value = value.reshape(per_head, tok // per_head, width)
                where = pl.ds((which * heads + h) * per_head, per_head)
                if slot == 0:
                    own[where] = value
                else:
                    give[slot - 1, where] = value.astype(BF)
        dq_ref[h] = dq_t.T.astype(BF)
        return carry

    lax.fori_loop(0, heads, differentiate, 0)

    swap_pair = remote(give.at[0], got.at[0], pair_send.at[2], pair_recv.at[2], sibling)
    swap_term = remote(give.at[2], got.at[1], pair_send.at[3], pair_recv.at[3], sibling)
    swap_term.start()
    swap_pair.start()
    swap_term.wait_recv()
    both_cores = give[1].astype(F32) + got[1].astype(F32)
    give[1] = both_cores.astype(BF)

    spread(give.at[1], in3, 2)

    pp_swap = []
    for t in range(2):
        att_swap[t].wait_recv()
        both = nn(att[side_rows[t]], w[near[1 - t]]) + nn(att_m[t], neighbour_w(t, 1))
        pp_out[t] = both.astype(BF)
        pp_swap.append(to_near(pp_out.at[t], pp_in.at[t], 6 + t, 1 - t))
        pp_swap[t].start()
    for t in range(2):
        g_acc[t] = nn(att[side_rows[t]], w[hi]) + nn(att_m[t], neighbour_w(t, 0))

    all_arrived(in3, 2)
    forward(in3, inv_ref, out3, back, 3)

    swap_pair.wait_recv()
    for t in range(2):
        pp_swap[t].wait_recv()
        proj_ref[side_rows[t]] = (g_acc[t] + pp_in[t].astype(F32)).astype(BF)

    all_arrived(back, 3)

    def finish(h, carry):
        for which, ref in ((0, dk_ref), (1, dv_ref)):
            where = pl.ds((which * heads + h) * per_head, per_head)
            remote_sum = (back[where].astype(F32) + got[0, where].astype(F32)).astype(BF)
            total = own[where] + remote_sum.astype(F32)
            ref[h] = total.astype(BF).reshape(tok, width)
        return carry

    lax.fori_loop(0, heads, finish, 0)

    for phase, ref in enumerate((kv.at[0], out1, give.at[1], out3)):
        arrived(ref.at[pl.ds(0, chips - 1)], a2a_send.at[phase])
    for axis in range(3):
        arrived(wx_stage_span(axis), wx_send.at[1 + axis])
    for copy in (
        [swap_own, swap_partner, swap_pair, swap_term, swap_wx, wx_cross]
        + cot_swap + gp_swap + att_swap + pp_swap
    ):
        copy.wait_send()


def per_device(queries, key_vectors, value_vectors, block_perm, out_weight, out_cotangent):
    chips = lax.axis_size("seq") // 2
    groups = lax.axis_size("head")
    heads, tok, width = queries.shape
    rows = 2 * heads * tok // chips
    cols = out_cotangent.shape[1]
    blocks = lax.iota(jnp.int32, chips)
    inverse = jnp.sum(
        jnp.where(block_perm[:, None, :] == blocks[None, :, None], blocks[None, None, :], 0), axis=2
    )
    in_hbm = pl.BlockSpec(memory_space=pltpu.HBM)
    smem = pl.BlockSpec(memory_space=pltpu.SMEM)
    vmem = pl.BlockSpec(memory_space=pltpu.VMEM)
    mat = jax.ShapeDtypeStruct((heads, tok, width), BF)
    pieces = (chips, rows, width)
    sides = (2, tok // 2, cols)
    flat = heads * width
    dma = pltpu.SemaphoreType.DMA
    scratch = [
        pltpu.VMEM((4,) + pieces, BF),
        pltpu.VMEM((heads, tok, width), BF),
        pltpu.VMEM((groups, flat, cols), BF),
        pltpu.VMEM((2, chips, 2 * flat // chips, cols), BF),
        pltpu.VMEM((tok, cols), BF),
        pltpu.VMEM(sides, BF),
        pltpu.VMEM((2, tok // 2, flat), BF),
        pltpu.VMEM((2, tok // 2, flat), BF),
        pltpu.VMEM((2, tok // 2, max(flat, cols)), F32),
        pltpu.VMEM(pieces, BF),
        pltpu.VMEM(pieces, BF),
        pltpu.VMEM(pieces, BF),
        pltpu.VMEM(pieces, BF),
        pltpu.VMEM(pieces, BF),
        pltpu.VMEM((heads, 4, tok, tok), BF),
        pltpu.VMEM((tok, flat), BF),
        pltpu.VMEM((2, tok // 2, flat), BF),
        pltpu.VMEM((heads, width, tok), BF),
        pltpu.VMEM((heads, tok, width), BF),
        pltpu.VMEM(sides, BF),
        pltpu.VMEM(sides, BF),
        pltpu.VMEM(pieces, F32),
        pltpu.VMEM((3,) + pieces, BF),
        pltpu.VMEM((2,) + pieces, BF),
        dma((8,)), dma((4,)), dma((4,)), dma((5,)), dma((5,)), dma((4,)), dma((4,)), dma((8,)), dma((8,)),
    ]
    return pl.pallas_call(
        functools.partial(kernel, (heads, tok, width, chips, groups)),
        out_shape=(jax.ShapeDtypeStruct((tok, cols), BF), mat, mat, mat),
        in_specs=[smem, smem] + [in_hbm] * 5,
        out_specs=(vmem,) * 4,
        scratch_shapes=scratch,
        compiler_params=pltpu.CompilerParams(
            collective_id=0, has_side_effects=True, vmem_limit_bytes=60 << 20
        ),
    )(
        block_perm,
        inverse,
        queries,
        key_vectors.reshape(chips // 2, rows, width),
        value_vectors.reshape(chips // 2, rows, width),
        out_weight.reshape(heads * width, -1),
        out_cotangent,
    )


def solution(mesh):
    return jax.shard_map(
        per_device,
        mesh=mesh,
        in_specs=(
            P("head", "seq", None),
            P("head", "seq", None),
            P("head", "seq", None),
            P("head", None),
            P("head", None, None),
            P("seq", "head"),
        ),
        out_specs=(
            P("seq", "head"),
            P("head", "seq", None),
            P("head", "seq", None),
            P("head", "seq", None),
        ),
        check_vma=False,
    )
```

```python
import functools
import math

import jax
import jax.numpy as jnp
from jax import lax
from jax.experimental import pallas as pl
from jax.experimental.pallas import tpu as pltpu
from jax.sharding import PartitionSpec as P

MESH = pl.DeviceIdType.MESH
BF = jnp.bfloat16
F32 = jnp.float32


def nn(a, b):
    return lax.dot_general(a, b, (((1,), (0,)), ((), ())), preferred_element_type=F32)


def nt(a, b):
    return lax.dot_general(a, b, (((1,), (1,)), ((), ())), preferred_element_type=F32)


def tn(a, b):
    return lax.dot_general(a, b, (((0,), (0,)), ((), ())), preferred_element_type=F32)


def digits(chips):
    side = round(chips ** (1 / 3))
    return (side * side, side, 1), side


def peer_chip(me, step, chips):
    units, side = digits(chips)
    out = 0
    for unit in units:
        digit = lax.rem(lax.div(me, unit), side) + lax.rem(lax.div(step, unit), side)
        out = out + unit * lax.rem(digit, side)
    return out


def kernel(
    dims,
    perm_ref, q_hbm, k_hbm, v_hbm, w_hbm, cot_hbm,
    proj_ref, dq_ref, dk_ref, dv_ref,
    inv_row, inv_ref, kv, q, w, wx, cot, cot_m, gp_out, gp_in, g_acc,
    in1, out1, in3, out3, back, prob, att, att_m, att_t, grad, pp_out, pp_in,
    own, give, got,
    load_sem, a2a_send, a2a_recv, pair_send, pair_recv, wx_send, wx_recv, hd_send, hd_recv,
):
    heads, tok, width, chips, groups = dims
    seq = lax.axis_index("seq")
    hi = lax.axis_index("head")
    core = lax.rem(seq, 2)
    me = lax.div(seq, 2)
    sibling = {"seq": me * 2 + 1 - core}
    near = (hi + 1 - 2 * lax.rem(hi, 2), groups - 1 - hi)
    per_head = chips // (2 * heads)
    mid = tok // 2
    side_rows = (pl.ds(0, mid), pl.ds(mid, mid))
    my_head = lax.rem(lax.div(me, per_head), heads)
    scale = 1.0 / math.sqrt(width)

    def on_chip(p):
        return {"seq": p * 2 + core}

    def remote(src, dst, send, recv, where):
        return pltpu.make_async_remote_copy(
            src_ref=src, dst_ref=dst, send_sem=send, recv_sem=recv,
            device_id=where, device_id_type=MESH,
        )

    def arrived(ref, sem):
        pltpu.make_async_copy(ref, ref, sem).wait()

    half = chips // 2
    load_k = pltpu.make_async_copy(k_hbm, kv.at[0, pl.ds(0, half)], load_sem.at[0])
    load_v = pltpu.make_async_copy(v_hbm, kv.at[0, pl.ds(half, half)], load_sem.at[1])
    load_cot = pltpu.make_async_copy(cot_hbm, cot, load_sem.at[2])
    load_q = pltpu.make_async_copy(q_hbm, q, load_sem.at[3])
    cols = cot_hbm.shape[1]
    load_w = [
        pltpu.make_async_copy(w_hbm.at[:, pl.ds(c * cols, cols)], w.at[c], load_sem.at[4 + c])
        for c in range(groups)
    ]
    for copy in [load_k, load_v] + load_w + [load_cot, load_q]:
        copy.start()

    barrier = pltpu.get_barrier_semaphore()

    def greet(step, carry):
        pl.semaphore_signal(
            barrier, inc=1, device_id=on_chip(peer_chip(me, step, chips)), device_id_type=MESH
        )
        return carry

    lax.fori_loop(1, chips, greet, 0)
    for where in (sibling, {"head": near[0]}, {"head": near[1]}):
        pl.semaphore_signal(barrier, inc=1, device_id=where, device_id_type=MESH)
    for copy in [load_k, load_v] + load_w + [load_cot, load_q]:
        copy.wait()
    pl.semaphore_wait(barrier, chips - 1 + 3)

    units, edge = digits(chips)
    x, y, z = (lax.rem(lax.div(me, unit), edge) for unit in units)
    wx_rows = wx.shape[4]
    blocks = chips // 2
    giver = near[0] + core * (near[1] - near[0])
    opposite = groups - 1 - near[0]
    block = lax.div(me, blocks)
    column = giver + block * (opposite - giver)
    row = pl.ds(pl.multiple_of(lax.rem(me, blocks) * wx_rows, wx_rows), wx_rows)
    mine = wx.at[core]
    wx_cross = remote(
        w.at[column, row], mine.at[x, y, z], wx_send.at[0], wx_recv.at[0], {"head": giver}
    )
    wx_cross.start()

    def wx_share(have, axis, sem):
        unit, digit = units[axis], (x, y, z)[axis]
        for j in range(1, edge):
            p = me + (lax.rem(digit + j, edge) - digit) * unit
            remote(have, have, wx_send.at[sem], wx_recv.at[sem], on_chip(p)).start()

    low_z, high_z = pl.ds(0, edge // 2), pl.ds(edge // 2, edge // 2)
    others = pl.ds(0, edge - 1)
    wx_spans = (
        mine.at[0, 0, others],
        mine.at[0, others, low_z], mine.at[others, 0, low_z],
        mine.at[others, :, low_z], mine.at[:, others, low_z],
    )

    def wx_wait(sems, index):
        for sem in index:
            arrived(wx_spans[sem - 1], sems.at[sem])

    def wx_start():
        wx_share(mine.at[x, y, z], 2, 1)

    def wx_first():
        wx_wait(wx_recv, (1,))
        wx_share(mine.at[x, y, low_z], 1, 2)
        wx_share(mine.at[x, y, high_z], 0, 3)

    def wx_end_first():
        wx_wait(wx_recv, (2, 3))

    def wx_second():
        wx_share(mine.at[x, :, low_z], 0, 4)
        wx_share(mine.at[:, y, high_z], 1, 5)

    def spread(src, dst, phase):
        def body(step, carry):
            p = peer_chip(me, step, chips)
            remote(src.at[p], dst.at[me], a2a_send.at[phase], a2a_recv.at[phase], on_chip(p)).start()
            return carry

        lax.fori_loop(1, chips, body, 0)
        dst[me] = src[me]

    def forward(src, table, row, out, dst, phase):
        def body(step, carry):
            p = peer_chip(me, step, chips)
            out[p] = src[table[row, p]]
            remote(out.at[p], dst.at[me], a2a_send.at[phase], a2a_recv.at[phase], on_chip(p)).start()
            return carry

        lax.fori_loop(1, chips, body, 0)
        dst[me] = src[table[row, me]]

    def invert():
        lane = lax.broadcasted_iota(jnp.int32, (8, 128), 1)

        def body(b, row):
            return jnp.where(lane == perm_ref[my_head, b], b, row)

        inv_row[...] = lax.fori_loop(0, chips, body, jnp.zeros((8, 128), jnp.int32))
        copy = pltpu.make_async_copy(inv_row, inv_ref, load_sem.at[8])
        copy.start()
        copy.wait()

    def all_arrived(dst, phase):
        arrived(dst.at[pl.ds(0, chips - 1)], a2a_recv.at[phase])

    def to_near(src, dst, slot, side):
        return remote(src, dst, hd_send.at[slot], hd_recv.at[slot], {"head": near[side]})

    spread(kv.at[0], in1, 0)
    wx_cross.wait_recv()
    wx_start()
    swap_own = remote(kv.at[0], kv.at[1], pair_send.at[0], pair_recv.at[0], sibling)
    swap_own.start()
    cot_swap = [to_near(cot.at[side_rows[t]], cot_m.at[t], t, t) for t in range(2)]
    for copy in cot_swap:
        copy.start()

    wx_first()
    all_arrived(in1, 0)
    forward(in1, perm_ref, my_head, out1, kv.at[2], 1)
    wx_end_first()
    wx_second()
    invert()

    def neighbour_w(source, which):
        value = wx[source, pl.ds(which * (edge // 2), edge // 2)]
        return value.reshape(blocks * wx_rows, cols)

    for t in range(2):
        cot_swap[t].wait_recv()
        g_acc[t] = nt(cot[side_rows[t]], w[hi]) + nt(cot_m[t], w[near[t]])

    wx_wait(wx_recv, (4, 5))
    swap_wx = remote(wx.at[core], wx.at[core], pair_send.at[4], pair_recv.at[4], sibling)
    swap_wx.start()
    swap_wx.wait_recv()
    gp_swap = []
    for t in range(2):
        both = nt(cot[side_rows[t]], neighbour_w(1 - t, 0)) + nt(cot_m[t], neighbour_w(1 - t, 1))
        gp_out[t] = both.astype(BF)
        gp_swap.append(to_near(gp_out.at[t], gp_in.at[t], 2 + t, 1 - t))
        gp_swap[t].start()

    all_arrived(kv.at[2], 1)
    swap_partner = remote(kv.at[2], kv.at[3], pair_send.at[1], pair_recv.at[1], sibling)
    swap_partner.start()
    swap_own.wait_recv()
    swap_partner.wait_recv()

    def rows_of(slot, which, h):
        piece = kv[slot, pl.ds((which * heads + h) * per_head, per_head)]
        return piece.reshape(tok, width)

    def attend(h, carry):
        q_h = q[h]
        scores = [nt(rows_of(slot, 0, h), q_h) for slot in range(4)]
        top_score = functools.reduce(
            jnp.maximum, [jnp.max(s, axis=0, keepdims=True) for s in scores]
        )
        weights = [jnp.exp2((s - top_score) * (scale * math.log2(math.e))) for s in scores]
        total = functools.reduce(
            jnp.add, [jnp.sum(e, axis=0, keepdims=True) for e in weights]
        )
        inverse = 1.0 / total
        acc = None
        for slot in range(4):
            low = (weights[slot] * inverse).astype(BF)
            prob[h, slot] = low
            term = tn(rows_of(slot, 1, h), low)
            acc = term if acc is None else acc + term
        low = acc.astype(BF)
        att_t[h] = low
        att[:, pl.ds(pl.multiple_of(h * width, width), width)] = low.T
        return carry

    lax.fori_loop(0, heads, attend, 0)

    att_swap = [to_near(att.at[side_rows[t]], att_m.at[t], 4 + t, t) for t in range(2)]
    for copy in att_swap:
        copy.start()

    for t in range(2):
        gp_swap[t].wait_recv()
        both = (g_acc[t] + gp_in[t].astype(F32)).astype(BF)
        for h in range(heads):
            grad[h, side_rows[t]] = both[:, h * width:(h + 1) * width]

    def differentiate(h, carry):
        q_h = q[h]
        grad_h = grad[h]
        delta = jnp.sum(
            grad_h.T.astype(F32) * att_t[h].astype(F32), axis=0, keepdims=True
        )
        dq_t = None
        for slot in range(4):
            low = prob[h, slot]
            d_prob = nt(rows_of(slot, 1, h), grad_h)
            d_score = (low.astype(F32) * ((d_prob - delta) * scale)).astype(BF)
            term = tn(rows_of(slot, 0, h), d_score)
            dq_t = term if dq_t is None else dq_t + term
            d_key = nn(d_score, q_h)
            d_value = nn(low, grad_h)
            for which, value in ((0, d_key), (1, d_value)):
                value = value.reshape(per_head, tok // per_head, width)
                where = pl.ds((which * heads + h) * per_head, per_head)
                if slot == 0:
                    own[where] = value
                else:
                    give[slot - 1, where] = value.astype(BF)
        dq_ref[h] = dq_t.T.astype(BF)
        return carry

    lax.fori_loop(0, heads, differentiate, 0)

    swap_pair = remote(give.at[0], got.at[0], pair_send.at[2], pair_recv.at[2], sibling)
    swap_term = remote(give.at[2], got.at[1], pair_send.at[3], pair_recv.at[3], sibling)
    swap_term.start()
    swap_pair.start()
    swap_term.wait_recv()
    both_cores = give[1].astype(F32) + got[1].astype(F32)
    give[1] = both_cores.astype(BF)

    spread(give.at[1], in3, 2)

    pp_swap = []
    for t in range(2):
        att_swap[t].wait_recv()
        both = nn(att[side_rows[t]], w[near[1 - t]]) + nn(att_m[t], neighbour_w(t, 1))
        pp_out[t] = both.astype(BF)
        pp_swap.append(to_near(pp_out.at[t], pp_in.at[t], 6 + t, 1 - t))
        pp_swap[t].start()
    for t in range(2):
        g_acc[t] = nn(att[side_rows[t]], w[hi]) + nn(att_m[t], neighbour_w(t, 0))

    all_arrived(in3, 2)
    forward(in3, inv_ref, 0, out3, back, 3)

    swap_pair.wait_recv()
    for t in range(2):
        pp_swap[t].wait_recv()
        proj_ref[side_rows[t]] = (g_acc[t] + pp_in[t].astype(F32)).astype(BF)

    all_arrived(back, 3)

    def finish(h, carry):
        for which, ref in ((0, dk_ref), (1, dv_ref)):
            where = pl.ds((which * heads + h) * per_head, per_head)
            remote_sum = (back[where].astype(F32) + got[0, where].astype(F32)).astype(BF)
            total = own[where] + remote_sum.astype(F32)
            ref[h] = total.astype(BF).reshape(tok, width)
        return carry

    lax.fori_loop(0, heads, finish, 0)

    for phase, ref in enumerate((kv.at[0], out1, give.at[1], out3)):
        arrived(ref.at[pl.ds(0, chips - 1)], a2a_send.at[phase])
    wx_wait(wx_send, (1, 2, 3, 4, 5))
    for copy in (
        [swap_own, swap_partner, swap_pair, swap_term, swap_wx, wx_cross]
        + cot_swap + gp_swap + att_swap + pp_swap
    ):
        copy.wait_send()


def hand_out(*refs):
    for source, target in zip(refs[:4], refs[4:]):
        target[...] = source[...]


def per_device(queries, key_vectors, value_vectors, block_perm, out_weight, out_cotangent):
    chips = lax.axis_size("seq") // 2
    groups = lax.axis_size("head")
    heads, tok, width = queries.shape
    rows = 2 * heads * tok // chips
    cols = out_cotangent.shape[1]
    in_hbm = pl.BlockSpec(memory_space=pltpu.HBM)
    smem = pl.BlockSpec(memory_space=pltpu.SMEM)
    vmem = pl.BlockSpec(memory_space=pltpu.VMEM)
    mat = jax.ShapeDtypeStruct((heads, tok, width), BF)
    pieces = (chips, rows, width)
    sides = (2, tok // 2, cols)
    flat = heads * width
    edge = digits(chips)[1]
    dma = pltpu.SemaphoreType.DMA
    scratch = [
        pltpu.VMEM((8, 128), jnp.int32),
        pltpu.SMEM((8, 128), jnp.int32),
        pltpu.VMEM((4,) + pieces, BF),
        pltpu.VMEM((heads, tok, width), BF),
        pltpu.VMEM((groups, flat, cols), BF),
        pltpu.VMEM((2, edge, edge, edge, 2 * flat // chips, cols), BF),
        pltpu.VMEM((tok, cols), BF),
        pltpu.VMEM(sides, BF),
        pltpu.VMEM((2, tok // 2, flat), BF),
        pltpu.VMEM((2, tok // 2, flat), BF),
        pltpu.VMEM((2, tok // 2, max(flat, cols)), F32),
        pltpu.VMEM(pieces, BF),
        pltpu.VMEM(pieces, BF),
        pltpu.VMEM(pieces, BF),
        pltpu.VMEM(pieces, BF),
        pltpu.VMEM(pieces, BF),
        pltpu.VMEM((heads, 4, tok, tok), BF),
        pltpu.VMEM((tok, flat), BF),
        pltpu.VMEM((2, tok // 2, flat), BF),
        pltpu.VMEM((heads, width, tok), BF),
        pltpu.VMEM((heads, tok, width), BF),
        pltpu.VMEM(sides, BF),
        pltpu.VMEM(sides, BF),
        pltpu.VMEM(pieces, F32),
        pltpu.VMEM((3,) + pieces, BF),
        pltpu.VMEM((2,) + pieces, BF),
        dma((9,)), dma((4,)), dma((4,)), dma((5,)), dma((5,)), dma((6,)), dma((6,)), dma((8,)), dma((8,)),
    ]
    results = pl.pallas_call(
        functools.partial(kernel, (heads, tok, width, chips, groups)),
        out_shape=(jax.ShapeDtypeStruct((tok, cols), BF), mat, mat, mat),
        in_specs=[smem] + [in_hbm] * 5,
        out_specs=(vmem,) * 4,
        scratch_shapes=scratch,
        compiler_params=pltpu.CompilerParams(
            collective_id=0, has_side_effects=True, vmem_limit_bytes=60 << 20
        ),
    )(
        block_perm,
        queries,
        key_vectors.reshape(chips // 2, rows, width),
        value_vectors.reshape(chips // 2, rows, width),
        out_weight.reshape(heads * width, -1),
        out_cotangent,
    )
    shapes = (jax.ShapeDtypeStruct((tok, cols), BF), mat, mat, mat)
    return pl.pallas_call(
        hand_out,
        out_shape=shapes,
        in_specs=[vmem] * 4,
        out_specs=(vmem,) * 4,
    )(*results)


def solution(mesh):
    return jax.shard_map(
        per_device,
        mesh=mesh,
        in_specs=(
            P("head", "seq", None),
            P("head", "seq", None),
            P("head", "seq", None),
            P("head", None),
            P("head", None, None),
            P("seq", "head"),
        ),
        out_specs=(
            P("seq", "head"),
            P("head", "seq", None),
            P("head", "seq", None),
            P("head", "seq", None),
        ),
        check_vma=False,
    )
```

```python
import functools
import math

import jax
import jax.numpy as jnp
from jax import lax
from jax.experimental import pallas as pl
from jax.experimental.pallas import tpu as pltpu
from jax.sharding import PartitionSpec as P

MESH = pl.DeviceIdType.MESH
BF = jnp.bfloat16
F32 = jnp.float32


def nn(a, b):
    return lax.dot_general(a, b, (((1,), (0,)), ((), ())), preferred_element_type=F32)


def nt(a, b):
    return lax.dot_general(a, b, (((1,), (1,)), ((), ())), preferred_element_type=F32)


def tn(a, b):
    return lax.dot_general(a, b, (((0,), (0,)), ((), ())), preferred_element_type=F32)


def digits(chips):
    side = round(chips ** (1 / 3))
    return (side * side, side, 1), side


def peer_chip(me, step, chips):
    units, side = digits(chips)
    out = 0
    for unit in units:
        digit = lax.rem(lax.div(me, unit), side) + lax.rem(lax.div(step, unit), side)
        out = out + unit * lax.rem(digit, side)
    return out


def kernel(
    dims,
    perm_ref, q_hbm, k_hbm, v_hbm, w_hbm, cot_hbm,
    proj_ref, dq_ref, dk_ref, dv_ref,
    inv_row, inv_ref, kv, q, w, wx, cot, cot_m, gp_out, gp_in, g_acc,
    in1, out1, in3, out3, back, prob, att, att_m, att_t, grad, pp_out, pp_in,
    own, give, got,
    load_sem, a2a_send, a2a_recv, pair_send, pair_recv, wx_send, wx_recv, hd_send, hd_recv,
):
    heads, tok, width, chips, groups = dims
    seq = lax.axis_index("seq")
    hi = lax.axis_index("head")
    core = lax.rem(seq, 2)
    me = lax.div(seq, 2)
    sibling = {"seq": me * 2 + 1 - core}
    near = (hi + 1 - 2 * lax.rem(hi, 2), groups - 1 - hi)
    per_head = chips // (2 * heads)
    mid = tok // 2
    side_rows = (pl.ds(0, mid), pl.ds(mid, mid))
    my_head = lax.rem(lax.div(me, per_head), heads)
    scale = 1.0 / math.sqrt(width)

    def on_chip(p):
        return {"seq": p * 2 + core}

    def remote(src, dst, send, recv, where):
        return pltpu.make_async_remote_copy(
            src_ref=src, dst_ref=dst, send_sem=send, recv_sem=recv,
            device_id=where, device_id_type=MESH,
        )

    def arrived(ref, sem):
        pltpu.make_async_copy(ref, ref, sem).wait()

    half = chips // 2
    load_k = pltpu.make_async_copy(k_hbm, kv.at[0, pl.ds(0, half)], load_sem.at[0])
    load_v = pltpu.make_async_copy(v_hbm, kv.at[0, pl.ds(half, half)], load_sem.at[1])
    load_cot = pltpu.make_async_copy(cot_hbm, cot, load_sem.at[2])
    load_q = pltpu.make_async_copy(q_hbm, q, load_sem.at[3])
    cols = cot_hbm.shape[1]
    load_w = [
        pltpu.make_async_copy(w_hbm.at[:, pl.ds(c * cols, cols)], w.at[c], load_sem.at[4 + c])
        for c in range(groups)
    ]
    for copy in [load_k, load_v] + load_w + [load_cot, load_q]:
        copy.start()

    barrier = pltpu.get_barrier_semaphore()

    def greet(step, carry):
        pl.semaphore_signal(
            barrier, inc=1, device_id=on_chip(peer_chip(me, step, chips)), device_id_type=MESH
        )
        return carry

    lax.fori_loop(1, chips, greet, 0)
    for where in (sibling, {"head": near[0]}, {"head": near[1]}):
        pl.semaphore_signal(barrier, inc=1, device_id=where, device_id_type=MESH)
    for copy in [load_k, load_v] + load_w + [load_cot, load_q]:
        copy.wait()
    pl.semaphore_wait(barrier, chips - 1 + 3)

    units, edge = digits(chips)
    x, y, z = (lax.rem(lax.div(me, unit), edge) for unit in units)
    wx_rows = wx.shape[4]
    blocks = chips // 2
    giver = near[0] + core * (near[1] - near[0])
    opposite = groups - 1 - near[0]
    block = lax.div(me, blocks)
    column = giver + block * (opposite - giver)
    row = pl.ds(pl.multiple_of(lax.rem(me, blocks) * wx_rows, wx_rows), wx_rows)
    mine = wx.at[core]
    wx_cross = remote(
        w.at[column, row], mine.at[x, y, z], wx_send.at[0], wx_recv.at[0], {"head": giver}
    )
    wx_cross.start()

    def wx_share(have, axis, sem):
        unit, digit = units[axis], (x, y, z)[axis]
        for j in range(1, edge):
            p = me + (lax.rem(digit + j, edge) - digit) * unit
            remote(have, have, wx_send.at[sem], wx_recv.at[sem], on_chip(p)).start()

    low_z, high_z = pl.ds(0, edge // 2), pl.ds(edge // 2, edge // 2)
    others = pl.ds(0, edge - 1)
    wx_spans = (
        mine.at[0, 0, others],
        mine.at[0, others, low_z], mine.at[others, 0, low_z],
        mine.at[others, :, low_z], mine.at[:, others, low_z],
    )

    def wx_wait(sems, index):
        for sem in index:
            arrived(wx_spans[sem - 1], sems.at[sem])

    def wx_start():
        wx_share(mine.at[x, y, z], 2, 1)

    def wx_first():
        wx_wait(wx_recv, (1,))
        wx_share(mine.at[x, y, low_z], 1, 2)
        wx_share(mine.at[x, y, high_z], 0, 3)

    def wx_end_first():
        wx_wait(wx_recv, (2, 3))

    def wx_second():
        wx_share(mine.at[x, :, low_z], 0, 4)
        wx_share(mine.at[:, y, high_z], 1, 5)

    def spread(src, dst, phase):
        def body(step, carry):
            p = peer_chip(me, step, chips)
            remote(src.at[p], dst.at[me], a2a_send.at[phase], a2a_recv.at[phase], on_chip(p)).start()
            return carry

        lax.fori_loop(1, chips, body, 0)
        dst[me] = src[me]

    def forward(src, table, row, out, dst, phase):
        def body(step, carry):
            p = peer_chip(me, step, chips)
            out[p] = src[table[row, p]]
            remote(out.at[p], dst.at[me], a2a_send.at[phase], a2a_recv.at[phase], on_chip(p)).start()
            return carry

        lax.fori_loop(1, chips, body, 0)
        dst[me] = src[table[row, me]]

    def invert():
        lane = lax.broadcasted_iota(jnp.int32, (8, 128), 1)

        def body(b, row):
            return jnp.where(lane == perm_ref[my_head, b], b, row)

        inv_row[...] = lax.fori_loop(0, chips, body, jnp.zeros((8, 128), jnp.int32))
        copy = pltpu.make_async_copy(inv_row, inv_ref, load_sem.at[8])
        copy.start()
        copy.wait()

    def all_arrived(dst, phase):
        arrived(dst.at[pl.ds(0, chips - 1)], a2a_recv.at[phase])

    def to_near(src, dst, slot, side):
        return remote(src, dst, hd_send.at[slot], hd_recv.at[slot], {"head": near[side]})

    spread(kv.at[0], in1, 0)
    wx_cross.wait_recv()
    wx_start()
    swap_own = remote(kv.at[0], kv.at[1], pair_send.at[0], pair_recv.at[0], sibling)
    swap_own.start()
    cot_swap = [to_near(cot.at[side_rows[t]], cot_m.at[t], t, t) for t in range(2)]

    cot_swap[0].start()
    wx_first()
    all_arrived(in1, 0)
    forward(in1, perm_ref, my_head, out1, kv.at[2], 1)
    cot_swap[1].start()
    wx_end_first()
    wx_second()
    invert()

    def neighbour_w(source, which):
        value = wx[source, pl.ds(which * (edge // 2), edge // 2)]
        return value.reshape(blocks * wx_rows, cols)

    for t in range(2):
        cot_swap[t].wait_recv()
        g_acc[t] = nt(cot[side_rows[t]], w[hi]) + nt(cot_m[t], w[near[t]])

    wx_wait(wx_recv, (4, 5))
    swap_wx = remote(wx.at[core], wx.at[core], pair_send.at[4], pair_recv.at[4], sibling)
    swap_wx.start()
    all_arrived(kv.at[2], 1)
    swap_partner = remote(kv.at[2], kv.at[3], pair_send.at[1], pair_recv.at[1], sibling)
    swap_partner.start()
    swap_wx.wait_recv()
    gp_swap = []
    for t in range(2):
        both = nt(cot[side_rows[t]], neighbour_w(1 - t, 0)) + nt(cot_m[t], neighbour_w(1 - t, 1))
        gp_out[t] = both.astype(BF)
        gp_swap.append(to_near(gp_out.at[t], gp_in.at[t], 2 + t, 1 - t))
        gp_swap[t].start()

    swap_own.wait_recv()
    swap_partner.wait_recv()

    def rows_of(slot, which, h):
        piece = kv[slot, pl.ds((which * heads + h) * per_head, per_head)]
        return piece.reshape(tok, width)

    def attend(h, carry):
        q_h = q[h]
        scores = [nt(rows_of(slot, 0, h), q_h) for slot in range(4)]
        top_score = functools.reduce(
            jnp.maximum, [jnp.max(s, axis=0, keepdims=True) for s in scores]
        )
        weights = [jnp.exp2((s - top_score) * (scale * math.log2(math.e))) for s in scores]
        total = functools.reduce(
            jnp.add, [jnp.sum(e, axis=0, keepdims=True) for e in weights]
        )
        inverse = 1.0 / total
        acc = None
        for slot in range(4):
            low = (weights[slot] * inverse).astype(BF)
            prob[h, slot] = low
            term = tn(rows_of(slot, 1, h), low)
            acc = term if acc is None else acc + term
        low = acc.astype(BF)
        att_t[h] = low
        att[:, pl.ds(pl.multiple_of(h * width, width), width)] = low.T
        return carry

    lax.fori_loop(0, heads, attend, 0)

    att_swap = [to_near(att.at[side_rows[t]], att_m.at[t], 4 + t, t) for t in range(2)]
    for copy in att_swap:
        copy.start()

    for t in range(2):
        gp_swap[t].wait_recv()
        both = (g_acc[t] + gp_in[t].astype(F32)).astype(BF)
        for h in range(heads):
            grad[h, side_rows[t]] = both[:, h * width:(h + 1) * width]

    def differentiate(h, carry):
        q_h = q[h]
        grad_h = grad[h]
        delta = jnp.sum(
            grad_h.T.astype(F32) * att_t[h].astype(F32), axis=0, keepdims=True
        )
        dq_t = None
        for slot in range(4):
            low = prob[h, slot]
            d_prob = nt(rows_of(slot, 1, h), grad_h)
            d_score = (low.astype(F32) * ((d_prob - delta) * scale)).astype(BF)
            term = tn(rows_of(slot, 0, h), d_score)
            dq_t = term if dq_t is None else dq_t + term
            d_key = nn(d_score, q_h)
            d_value = nn(low, grad_h)
            for which, value in ((0, d_key), (1, d_value)):
                value = value.reshape(per_head, tok // per_head, width)
                where = pl.ds((which * heads + h) * per_head, per_head)
                if slot == 0:
                    own[where] = value
                else:
                    give[slot - 1, where] = value.astype(BF)
        dq_ref[h] = dq_t.T.astype(BF)
        return carry

    lax.fori_loop(0, heads, differentiate, 0)

    swap_pair = remote(give.at[0], got.at[0], pair_send.at[2], pair_recv.at[2], sibling)
    swap_term = remote(give.at[2], got.at[1], pair_send.at[3], pair_recv.at[3], sibling)
    swap_term.start()
    swap_pair.start()
    swap_term.wait_recv()
    both_cores = give[1].astype(F32) + got[1].astype(F32)
    give[1] = both_cores.astype(BF)

    spread(give.at[1], in3, 2)

    pp_swap = []
    for t in range(2):
        att_swap[t].wait_recv()
        both = nn(att[side_rows[t]], w[near[1 - t]]) + nn(att_m[t], neighbour_w(t, 1))
        pp_out[t] = both.astype(BF)
        pp_swap.append(to_near(pp_out.at[t], pp_in.at[t], 6 + t, 1 - t))
        pp_swap[t].start()
    for t in range(2):
        g_acc[t] = nn(att[side_rows[t]], w[hi]) + nn(att_m[t], neighbour_w(t, 0))

    all_arrived(in3, 2)
    forward(in3, inv_ref, 0, out3, back, 3)

    swap_pair.wait_recv()
    for t in range(2):
        pp_swap[t].wait_recv()
        proj_ref[side_rows[t]] = (g_acc[t] + pp_in[t].astype(F32)).astype(BF)

    all_arrived(back, 3)

    def finish(h, carry):
        for which, ref in ((0, dk_ref), (1, dv_ref)):
            where = pl.ds((which * heads + h) * per_head, per_head)
            remote_sum = (back[where].astype(F32) + got[0, where].astype(F32)).astype(BF)
            total = own[where] + remote_sum.astype(F32)
            ref[h] = total.astype(BF).reshape(tok, width)
        return carry

    lax.fori_loop(0, heads, finish, 0)

    for phase, ref in enumerate((kv.at[0], out1, give.at[1], out3)):
        arrived(ref.at[pl.ds(0, chips - 1)], a2a_send.at[phase])
    wx_wait(wx_send, (1, 2, 3, 4, 5))
    for copy in (
        [swap_own, swap_partner, swap_pair, swap_term, swap_wx, wx_cross]
        + cot_swap + gp_swap + att_swap + pp_swap
    ):
        copy.wait_send()


def hand_out(*refs):
    for source, target in zip(refs[:4], refs[4:]):
        target[...] = source[...]


def per_device(queries, key_vectors, value_vectors, block_perm, out_weight, out_cotangent):
    chips = lax.axis_size("seq") // 2
    groups = lax.axis_size("head")
    heads, tok, width = queries.shape
    rows = 2 * heads * tok // chips
    cols = out_cotangent.shape[1]
    in_hbm = pl.BlockSpec(memory_space=pltpu.HBM)
    smem = pl.BlockSpec(memory_space=pltpu.SMEM)
    vmem = pl.BlockSpec(memory_space=pltpu.VMEM)
    mat = jax.ShapeDtypeStruct((heads, tok, width), BF)
    pieces = (chips, rows, width)
    sides = (2, tok // 2, cols)
    flat = heads * width
    edge = digits(chips)[1]
    dma = pltpu.SemaphoreType.DMA
    scratch = [
        pltpu.VMEM((8, 128), jnp.int32),
        pltpu.SMEM((8, 128), jnp.int32),
        pltpu.VMEM((4,) + pieces, BF),
        pltpu.VMEM((heads, tok, width), BF),
        pltpu.VMEM((groups, flat, cols), BF),
        pltpu.VMEM((2, edge, edge, edge, 2 * flat // chips, cols), BF),
        pltpu.VMEM((tok, cols), BF),
        pltpu.VMEM(sides, BF),
        pltpu.VMEM((2, tok // 2, flat), BF),
        pltpu.VMEM((2, tok // 2, flat), BF),
        pltpu.VMEM((2, tok // 2, max(flat, cols)), F32),
        pltpu.VMEM(pieces, BF),
        pltpu.VMEM(pieces, BF),
        pltpu.VMEM(pieces, BF),
        pltpu.VMEM(pieces, BF),
        pltpu.VMEM(pieces, BF),
        pltpu.VMEM((heads, 4, tok, tok), BF),
        pltpu.VMEM((tok, flat), BF),
        pltpu.VMEM((2, tok // 2, flat), BF),
        pltpu.VMEM((heads, width, tok), BF),
        pltpu.VMEM((heads, tok, width), BF),
        pltpu.VMEM(sides, BF),
        pltpu.VMEM(sides, BF),
        pltpu.VMEM(pieces, F32),
        pltpu.VMEM((3,) + pieces, BF),
        pltpu.VMEM((2,) + pieces, BF),
        dma((9,)), dma((4,)), dma((4,)), dma((5,)), dma((5,)), dma((6,)), dma((6,)), dma((8,)), dma((8,)),
    ]
    results = pl.pallas_call(
        functools.partial(kernel, (heads, tok, width, chips, groups)),
        out_shape=(jax.ShapeDtypeStruct((tok, cols), BF), mat, mat, mat),
        in_specs=[smem] + [in_hbm] * 5,
        out_specs=(vmem,) * 4,
        scratch_shapes=scratch,
        compiler_params=pltpu.CompilerParams(
            collective_id=0, has_side_effects=True, vmem_limit_bytes=60 << 20
        ),
    )(
        block_perm,
        queries,
        key_vectors.reshape(chips // 2, rows, width),
        value_vectors.reshape(chips // 2, rows, width),
        out_weight.reshape(heads * width, -1),
        out_cotangent,
    )
    shapes = (jax.ShapeDtypeStruct((tok, cols), BF), mat, mat, mat)
    return pl.pallas_call(
        hand_out,
        out_shape=shapes,
        in_specs=[vmem] * 4,
        out_specs=(vmem,) * 4,
    )(*results)


def solution(mesh):
    return jax.shard_map(
        per_device,
        mesh=mesh,
        in_specs=(
            P("head", "seq", None),
            P("head", "seq", None),
            P("head", "seq", None),
            P("head", None),
            P("head", None, None),
            P("seq", "head"),
        ),
        out_specs=(
            P("seq", "head"),
            P("head", "seq", None),
            P("head", "seq", None),
            P("head", "seq", None),
        ),
        check_vma=False,
    )
```

```python
import functools
import math

import jax
import jax.numpy as jnp
from jax import lax
from jax.experimental import pallas as pl
from jax.experimental.pallas import tpu as pltpu
from jax.sharding import PartitionSpec as P

MESH = pl.DeviceIdType.MESH
BF = jnp.bfloat16
F32 = jnp.float32


def nn(a, b):
    return lax.dot_general(a, b, (((1,), (0,)), ((), ())), preferred_element_type=F32)


def nt(a, b):
    return lax.dot_general(a, b, (((1,), (1,)), ((), ())), preferred_element_type=F32)


def tn(a, b):
    return lax.dot_general(a, b, (((0,), (0,)), ((), ())), preferred_element_type=F32)


def digits(chips):
    side = round(chips ** (1 / 3))
    return (side * side, side, 1), side


def peer_chip(me, step, chips):
    units, side = digits(chips)
    out = 0
    for unit in units:
        digit = lax.rem(lax.div(me, unit), side) + lax.rem(lax.div(step, unit), side)
        out = out + unit * lax.rem(digit, side)
    return out


def kernel(
    dims,
    perm_ref, q_hbm, k_hbm, v_hbm, w_hbm, cot_hbm,
    proj_ref, dq_ref, dk_ref, dv_ref,
    inv_row, inv_ref, kv, q, w, wx, cot, cot_m, gp_out, gp_in, g_acc,
    in1, out1, in3, out3, back, prob, att, att_m, att_t, grad, pp_out, pp_in,
    own, give, got, dq_acc,
    load_sem, a2a_send, a2a_recv, pair_send, pair_recv, wx_send, wx_recv, hd_send, hd_recv,
):
    heads, tok, width, chips, groups = dims
    seq = lax.axis_index("seq")
    hi = lax.axis_index("head")
    core = lax.rem(seq, 2)
    me = lax.div(seq, 2)
    sibling = {"seq": me * 2 + 1 - core}
    near = (hi + 1 - 2 * lax.rem(hi, 2), groups - 1 - hi)
    per_head = chips // (2 * heads)
    mid = tok // 2
    side_rows = (pl.ds(0, mid), pl.ds(mid, mid))
    my_head = lax.rem(lax.div(me, per_head), heads)
    scale = 1.0 / math.sqrt(width)

    def on_chip(p):
        return {"seq": p * 2 + core}

    def remote(src, dst, send, recv, where):
        return pltpu.make_async_remote_copy(
            src_ref=src, dst_ref=dst, send_sem=send, recv_sem=recv,
            device_id=where, device_id_type=MESH,
        )

    def arrived(ref, sem):
        pltpu.make_async_copy(ref, ref, sem).wait()

    half = chips // 2
    load_k = pltpu.make_async_copy(k_hbm, kv.at[0, pl.ds(0, half)], load_sem.at[0])
    load_v = pltpu.make_async_copy(v_hbm, kv.at[0, pl.ds(half, half)], load_sem.at[1])
    load_cot = pltpu.make_async_copy(cot_hbm, cot, load_sem.at[2])
    load_q = pltpu.make_async_copy(q_hbm, q, load_sem.at[3])
    cols = cot_hbm.shape[1]
    load_w = [
        pltpu.make_async_copy(w_hbm.at[:, pl.ds(c * cols, cols)], w.at[c], load_sem.at[4 + c])
        for c in range(groups)
    ]
    for copy in [load_k, load_v] + load_w + [load_cot, load_q]:
        copy.start()

    barrier = pltpu.get_barrier_semaphore()

    def greet(step, carry):
        pl.semaphore_signal(
            barrier, inc=1, device_id=on_chip(peer_chip(me, step, chips)), device_id_type=MESH
        )
        return carry

    lax.fori_loop(1, chips, greet, 0)
    for where in (sibling, {"head": near[0]}, {"head": near[1]}):
        pl.semaphore_signal(barrier, inc=1, device_id=where, device_id_type=MESH)
    for copy in [load_k, load_v] + load_w + [load_cot, load_q]:
        copy.wait()
    pl.semaphore_wait(barrier, chips - 1 + 3)

    units, edge = digits(chips)
    x, y, z = (lax.rem(lax.div(me, unit), edge) for unit in units)
    wx_rows = wx.shape[4]
    blocks = chips // 2
    giver = near[0] + core * (near[1] - near[0])
    opposite = groups - 1 - near[0]
    block = lax.div(me, blocks)
    column = giver + block * (opposite - giver)
    row = pl.ds(pl.multiple_of(lax.rem(me, blocks) * wx_rows, wx_rows), wx_rows)
    mine = wx.at[core]
    wx_cross = remote(
        w.at[column, row], mine.at[x, y, z], wx_send.at[0], wx_recv.at[0], {"head": giver}
    )
    wx_cross.start()

    def wx_share(have, axis, sem):
        unit, digit = units[axis], (x, y, z)[axis]
        for j in range(1, edge):
            p = me + (lax.rem(digit + j, edge) - digit) * unit
            remote(have, have, wx_send.at[sem], wx_recv.at[sem], on_chip(p)).start()

    low_z, high_z = pl.ds(0, edge // 2), pl.ds(edge // 2, edge // 2)
    others = pl.ds(0, edge - 1)
    wx_spans = (
        mine.at[0, 0, others],
        mine.at[0, others, low_z], mine.at[others, 0, low_z],
        mine.at[others, :, low_z], mine.at[:, others, low_z],
    )

    def wx_wait(sems, index):
        for sem in index:
            arrived(wx_spans[sem - 1], sems.at[sem])

    def wx_start():
        wx_share(mine.at[x, y, z], 2, 1)

    def wx_first():
        wx_wait(wx_recv, (1,))
        wx_share(mine.at[x, y, low_z], 1, 2)
        wx_share(mine.at[x, y, high_z], 0, 3)

    def wx_end_first():
        wx_wait(wx_recv, (2, 3))

    def wx_second():
        wx_share(mine.at[x, :, low_z], 0, 4)
        wx_share(mine.at[:, y, high_z], 1, 5)

    def spread(src, dst, phase):
        def body(step, carry):
            p = peer_chip(me, step, chips)
            remote(src.at[p], dst.at[me], a2a_send.at[phase], a2a_recv.at[phase], on_chip(p)).start()
            return carry

        lax.fori_loop(1, chips, body, 0)
        dst[me] = src[me]

    def forward(src, table, row, out, dst, phase):
        def body(step, carry):
            p = peer_chip(me, step, chips)
            out[p] = src[table[row, p]]
            remote(out.at[p], dst.at[me], a2a_send.at[phase], a2a_recv.at[phase], on_chip(p)).start()
            return carry

        lax.fori_loop(1, chips, body, 0)
        dst[me] = src[table[row, me]]

    def invert():
        lane = lax.broadcasted_iota(jnp.int32, (8, 128), 1)

        def body(b, row):
            return jnp.where(lane == perm_ref[my_head, b], b, row)

        inv_row[...] = lax.fori_loop(0, chips, body, jnp.zeros((8, 128), jnp.int32))
        copy = pltpu.make_async_copy(inv_row, inv_ref, load_sem.at[8])
        copy.start()
        copy.wait()

    def all_arrived(dst, phase):
        arrived(dst.at[pl.ds(0, chips - 1)], a2a_recv.at[phase])

    def to_near(src, dst, slot, side):
        return remote(src, dst, hd_send.at[slot], hd_recv.at[slot], {"head": near[side]})

    spread(kv.at[0], in1, 0)
    wx_cross.wait_recv()
    wx_start()
    swap_own = remote(kv.at[0], kv.at[1], pair_send.at[0], pair_recv.at[0], sibling)
    swap_own.start()
    cot_swap = [to_near(cot.at[side_rows[t]], cot_m.at[t], t, t) for t in range(2)]

    cot_swap[0].start()
    wx_first()
    all_arrived(in1, 0)
    forward(in1, perm_ref, my_head, out1, kv.at[2], 1)
    cot_swap[1].start()
    wx_end_first()
    wx_second()
    invert()

    def neighbour_w(source, which):
        value = wx[source, pl.ds(which * (edge // 2), edge // 2)]
        return value.reshape(blocks * wx_rows, cols)

    for t in range(2):
        cot_swap[t].wait_recv()
        g_acc[t] = nt(cot[side_rows[t]], w[hi]) + nt(cot_m[t], w[near[t]])

    wx_wait(wx_recv, (4, 5))
    swap_wx = remote(wx.at[core], wx.at[core], pair_send.at[4], pair_recv.at[4], sibling)
    swap_wx.start()
    all_arrived(kv.at[2], 1)
    swap_partner = remote(kv.at[2], kv.at[3], pair_send.at[1], pair_recv.at[1], sibling)
    swap_partner.start()
    swap_wx.wait_recv()
    gp_swap = []
    for t in range(2):
        both = nt(cot[side_rows[t]], neighbour_w(1 - t, 0)) + nt(cot_m[t], neighbour_w(1 - t, 1))
        gp_out[t] = both.astype(BF)
        gp_swap.append(to_near(gp_out.at[t], gp_in.at[t], 2 + t, 1 - t))
        gp_swap[t].start()

    swap_own.wait_recv()
    swap_partner.wait_recv()

    def rows_of(slot, which, h):
        piece = kv[slot, pl.ds((which * heads + h) * per_head, per_head)]
        return piece.reshape(tok, width)

    def attend(h, carry):
        q_h = q[h]
        scores = [nt(rows_of(slot, 0, h), q_h) for slot in range(4)]
        top_score = functools.reduce(
            jnp.maximum, [jnp.max(s, axis=0, keepdims=True) for s in scores]
        )
        weights = [jnp.exp2((s - top_score) * (scale * math.log2(math.e))) for s in scores]
        total = functools.reduce(
            jnp.add, [jnp.sum(e, axis=0, keepdims=True) for e in weights]
        )
        inverse = 1.0 / total
        acc = None
        for slot in range(4):
            low = (weights[slot] * inverse).astype(BF)
            prob[h, slot] = low
            term = tn(rows_of(slot, 1, h), low)
            acc = term if acc is None else acc + term
        low = acc.astype(BF)
        att_t[h] = low
        att[:, pl.ds(pl.multiple_of(h * width, width), width)] = low.T
        return carry

    lax.fori_loop(0, heads, attend, 0)

    att_swap = [to_near(att.at[side_rows[t]], att_m.at[t], 4 + t, t) for t in range(2)]
    for copy in att_swap:
        copy.start()

    for t in range(2):
        gp_swap[t].wait_recv()
        both = (g_acc[t] + gp_in[t].astype(F32)).astype(BF)
        for h in range(heads):
            grad[h, side_rows[t]] = both[:, h * width:(h + 1) * width]

    def differentiate(h, slots):
        q_h = q[h]
        grad_h = grad[h]
        delta = jnp.sum(
            grad_h.T.astype(F32) * att_t[h].astype(F32), axis=0, keepdims=True
        )
        dq_t = None
        for slot in slots:
            low = prob[h, slot]
            d_prob = nt(rows_of(slot, 1, h), grad_h)
            d_score = (low.astype(F32) * ((d_prob - delta) * scale)).astype(BF)
            term = tn(rows_of(slot, 0, h), d_score)
            dq_t = term if dq_t is None else dq_t + term
            d_key = nn(d_score, q_h)
            d_value = nn(low, grad_h)
            for which, value in ((0, d_key), (1, d_value)):
                value = value.reshape(per_head, tok // per_head, width)
                where = pl.ds((which * heads + h) * per_head, per_head)
                if slot == 0:
                    own[where] = value
                else:
                    give[slot - 1, where] = value.astype(BF)
        return dq_t

    def partner_rows(h, carry):
        dq_acc[h] = differentiate(h, (3, 2))
        for which in range(2):
            where = pl.ds((which * heads + h) * per_head, per_head)
            remote(
                give.at[2, where], got.at[1, where], pair_send.at[3], pair_recv.at[3], sibling
            ).start()
        return carry

    def block_rows(h, carry):
        dq_t = dq_acc[h] + differentiate(h, (1, 0))
        dq_ref[h] = dq_t.T.astype(BF)
        return carry

    lax.fori_loop(0, heads, partner_rows, 0)
    swap_pair = remote(give.at[0], got.at[0], pair_send.at[2], pair_recv.at[2], sibling)
    arrived(got.at[1], pair_recv.at[3])
    both_cores = give[1].astype(F32) + got[1].astype(F32)
    give[1] = both_cores.astype(BF)

    spread(give.at[1], in3, 2)
    lax.fori_loop(0, heads, block_rows, 0)
    swap_pair.start()

    pp_swap = []
    for t in range(2):
        att_swap[t].wait_recv()
        both = nn(att[side_rows[t]], w[near[1 - t]]) + nn(att_m[t], neighbour_w(t, 1))
        pp_out[t] = both.astype(BF)
        pp_swap.append(to_near(pp_out.at[t], pp_in.at[t], 6 + t, 1 - t))
        pp_swap[t].start()
    for t in range(2):
        g_acc[t] = nn(att[side_rows[t]], w[hi]) + nn(att_m[t], neighbour_w(t, 0))

    all_arrived(in3, 2)
    forward(in3, inv_ref, 0, out3, back, 3)

    swap_pair.wait_recv()
    for t in range(2):
        pp_swap[t].wait_recv()
        proj_ref[side_rows[t]] = (g_acc[t] + pp_in[t].astype(F32)).astype(BF)

    all_arrived(back, 3)

    def finish(h, carry):
        for which, ref in ((0, dk_ref), (1, dv_ref)):
            where = pl.ds((which * heads + h) * per_head, per_head)
            remote_sum = (back[where].astype(F32) + got[0, where].astype(F32)).astype(BF)
            total = own[where] + remote_sum.astype(F32)
            ref[h] = total.astype(BF).reshape(tok, width)
        return carry

    lax.fori_loop(0, heads, finish, 0)

    arrived(give.at[2], pair_send.at[3])
    for phase, ref in enumerate((kv.at[0], out1, give.at[1], out3)):
        arrived(ref.at[pl.ds(0, chips - 1)], a2a_send.at[phase])
    wx_wait(wx_send, (1, 2, 3, 4, 5))
    for copy in (
        [swap_own, swap_partner, swap_pair, swap_wx, wx_cross]
        + cot_swap + gp_swap + att_swap + pp_swap
    ):
        copy.wait_send()


def hand_out(*refs):
    for source, target in zip(refs[:4], refs[4:]):
        target[...] = source[...]


def per_device(queries, key_vectors, value_vectors, block_perm, out_weight, out_cotangent):
    chips = lax.axis_size("seq") // 2
    groups = lax.axis_size("head")
    heads, tok, width = queries.shape
    rows = 2 * heads * tok // chips
    cols = out_cotangent.shape[1]
    in_hbm = pl.BlockSpec(memory_space=pltpu.HBM)
    smem = pl.BlockSpec(memory_space=pltpu.SMEM)
    vmem = pl.BlockSpec(memory_space=pltpu.VMEM)
    mat = jax.ShapeDtypeStruct((heads, tok, width), BF)
    pieces = (chips, rows, width)
    sides = (2, tok // 2, cols)
    flat = heads * width
    edge = digits(chips)[1]
    dma = pltpu.SemaphoreType.DMA
    scratch = [
        pltpu.VMEM((8, 128), jnp.int32),
        pltpu.SMEM((8, 128), jnp.int32),
        pltpu.VMEM((4,) + pieces, BF),
        pltpu.VMEM((heads, tok, width), BF),
        pltpu.VMEM((groups, flat, cols), BF),
        pltpu.VMEM((2, edge, edge, edge, 2 * flat // chips, cols), BF),
        pltpu.VMEM((tok, cols), BF),
        pltpu.VMEM(sides, BF),
        pltpu.VMEM((2, tok // 2, flat), BF),
        pltpu.VMEM((2, tok // 2, flat), BF),
        pltpu.VMEM((2, tok // 2, max(flat, cols)), F32),
        pltpu.VMEM(pieces, BF),
        pltpu.VMEM(pieces, BF),
        pltpu.VMEM(pieces, BF),
        pltpu.VMEM(pieces, BF),
        pltpu.VMEM(pieces, BF),
        pltpu.VMEM((heads, 4, tok, tok), BF),
        pltpu.VMEM((tok, flat), BF),
        pltpu.VMEM((2, tok // 2, flat), BF),
        pltpu.VMEM((heads, width, tok), BF),
        pltpu.VMEM((heads, tok, width), BF),
        pltpu.VMEM(sides, BF),
        pltpu.VMEM(sides, BF),
        pltpu.VMEM(pieces, F32),
        pltpu.VMEM((3,) + pieces, BF),
        pltpu.VMEM((2,) + pieces, BF),
        pltpu.VMEM((heads, width, tok), F32),
        dma((9,)), dma((4,)), dma((4,)), dma((5,)), dma((5,)), dma((6,)), dma((6,)), dma((8,)), dma((8,)),
    ]
    results = pl.pallas_call(
        functools.partial(kernel, (heads, tok, width, chips, groups)),
        out_shape=(jax.ShapeDtypeStruct((tok, cols), BF), mat, mat, mat),
        in_specs=[smem] + [in_hbm] * 5,
        out_specs=(vmem,) * 4,
        scratch_shapes=scratch,
        compiler_params=pltpu.CompilerParams(
            collective_id=0, has_side_effects=True, vmem_limit_bytes=60 << 20
        ),
    )(
        block_perm,
        queries,
        key_vectors.reshape(chips // 2, rows, width),
        value_vectors.reshape(chips // 2, rows, width),
        out_weight.reshape(heads * width, -1),
        out_cotangent,
    )
    shapes = (jax.ShapeDtypeStruct((tok, cols), BF), mat, mat, mat)
    return pl.pallas_call(
        hand_out,
        out_shape=shapes,
        in_specs=[vmem] * 4,
        out_specs=(vmem,) * 4,
    )(*results)


def solution(mesh):
    return jax.shard_map(
        per_device,
        mesh=mesh,
        in_specs=(
            P("head", "seq", None),
            P("head", "seq", None),
            P("head", "seq", None),
            P("head", None),
            P("head", None, None),
            P("seq", "head"),
        ),
        out_specs=(
            P("seq", "head"),
            P("head", "seq", None),
            P("head", "seq", None),
            P("head", "seq", None),
        ),
        check_vma=False,
    )
```

```python
import functools
import math

import jax
import jax.numpy as jnp
from jax import lax
from jax.experimental import pallas as pl
from jax.experimental.pallas import tpu as pltpu
from jax.sharding import PartitionSpec as P

MESH = pl.DeviceIdType.MESH
BF = jnp.bfloat16
F32 = jnp.float32


def nn(a, b):
    return lax.dot_general(a, b, (((1,), (0,)), ((), ())), preferred_element_type=F32)


def nt(a, b):
    return lax.dot_general(a, b, (((1,), (1,)), ((), ())), preferred_element_type=F32)


def tn(a, b):
    return lax.dot_general(a, b, (((0,), (0,)), ((), ())), preferred_element_type=F32)


def digits(chips):
    side = round(chips ** (1 / 3))
    return (side * side, side, 1), side


def peer_chip(me, step, chips):
    units, side = digits(chips)
    out = 0
    for unit in units:
        digit = lax.rem(lax.div(me, unit), side) + lax.rem(lax.div(step, unit), side)
        out = out + unit * lax.rem(digit, side)
    return out


def kernel(
    dims,
    perm_ref, q_hbm, k_hbm, v_hbm, w_hbm, cot_hbm,
    proj_ref, dq_ref, dk_ref, dv_ref,
    inv_row, inv_ref, kv, q, w, wx, cot, cot_m, gp_out, gp_in, g_acc,
    in1, out1, in3, out3, back, prob, att, att_m, att_t, grad, pp_out, pp_in,
    own, give, got, dq_acc,
    load_sem, a2a_send, a2a_recv, pair_send, pair_recv, wx_send, wx_recv, hd_send, hd_recv,
):
    heads, tok, width, chips, groups = dims
    seq = lax.axis_index("seq")
    hi = lax.axis_index("head")
    core = lax.rem(seq, 2)
    me = lax.div(seq, 2)
    sibling = {"seq": me * 2 + 1 - core}
    near = (hi + 1 - 2 * lax.rem(hi, 2), groups - 1 - hi)
    per_head = chips // (2 * heads)
    mid = tok // 2
    side_rows = (pl.ds(0, mid), pl.ds(mid, mid))
    my_head = lax.rem(lax.div(me, per_head), heads)
    scale = 1.0 / math.sqrt(width)

    def on_chip(p):
        return {"seq": p * 2 + core}

    def remote(src, dst, send, recv, where):
        return pltpu.make_async_remote_copy(
            src_ref=src, dst_ref=dst, send_sem=send, recv_sem=recv,
            device_id=where, device_id_type=MESH,
        )

    def arrived(ref, sem):
        pltpu.make_async_copy(ref, ref, sem).wait()

    half = chips // 2
    load_k = pltpu.make_async_copy(k_hbm, kv.at[0, pl.ds(0, half)], load_sem.at[0])
    load_v = pltpu.make_async_copy(v_hbm, kv.at[0, pl.ds(half, half)], load_sem.at[1])
    load_cot = pltpu.make_async_copy(cot_hbm, cot, load_sem.at[2])
    load_q = pltpu.make_async_copy(q_hbm, q, load_sem.at[3])
    cols = cot_hbm.shape[1]
    load_w = [
        pltpu.make_async_copy(w_hbm.at[:, pl.ds(c * cols, cols)], w.at[c], load_sem.at[4 + c])
        for c in range(groups)
    ]
    for copy in [load_k, load_v] + load_w + [load_cot, load_q]:
        copy.start()

    barrier = pltpu.get_barrier_semaphore()

    def greet(step, carry):
        pl.semaphore_signal(
            barrier, inc=1, device_id=on_chip(peer_chip(me, step, chips)), device_id_type=MESH
        )
        return carry

    lax.fori_loop(1, chips, greet, 0)
    for where in (sibling, {"head": near[0]}, {"head": near[1]}):
        pl.semaphore_signal(barrier, inc=1, device_id=where, device_id_type=MESH)
    for copy in [load_k, load_v] + load_w + [load_cot, load_q]:
        copy.wait()
    pl.semaphore_wait(barrier, chips - 1 + 3)

    units, edge = digits(chips)
    x, y, z = (lax.rem(lax.div(me, unit), edge) for unit in units)
    wx_rows = wx.shape[4]
    blocks = chips // 2
    giver = near[0] + core * (near[1] - near[0])
    opposite = groups - 1 - near[0]
    block = lax.div(me, blocks)
    column = giver + block * (opposite - giver)
    row = pl.ds(pl.multiple_of(lax.rem(me, blocks) * wx_rows, wx_rows), wx_rows)
    mine = wx.at[core]
    wx_cross = remote(
        w.at[column, row], mine.at[x, y, z], wx_send.at[0], wx_recv.at[0], {"head": giver}
    )
    wx_cross.start()

    def wx_share(have, axis, sem):
        unit, digit = units[axis], (x, y, z)[axis]
        for j in range(1, edge):
            p = me + (lax.rem(digit + j, edge) - digit) * unit
            remote(have, have, wx_send.at[sem], wx_recv.at[sem], on_chip(p)).start()

    low_z, high_z = pl.ds(0, edge // 2), pl.ds(edge // 2, edge // 2)
    others = pl.ds(0, edge - 1)
    wx_spans = (
        mine.at[0, 0, others],
        mine.at[0, others, low_z], mine.at[others, 0, low_z],
        mine.at[others, :, low_z], mine.at[:, others, low_z],
    )

    def wx_wait(sems, index):
        for sem in index:
            arrived(wx_spans[sem - 1], sems.at[sem])

    def wx_start():
        wx_share(mine.at[x, y, z], 2, 1)

    def wx_first():
        wx_wait(wx_recv, (1,))
        wx_share(mine.at[x, y, low_z], 1, 2)
        wx_share(mine.at[x, y, high_z], 0, 3)

    def wx_end_first():
        wx_wait(wx_recv, (2, 3))

    def wx_second():
        wx_share(mine.at[x, :, low_z], 0, 4)
        wx_share(mine.at[:, y, high_z], 1, 5)

    def spread(src, dst, phase):
        def body(step, carry):
            p = peer_chip(me, step, chips)
            remote(src.at[p], dst.at[me], a2a_send.at[phase], a2a_recv.at[phase], on_chip(p)).start()
            return carry

        lax.fori_loop(1, chips, body, 0)
        dst[me] = src[me]

    def forward(src, table, row, out, dst, phase):
        def body(step, carry):
            p = peer_chip(me, step, chips)
            out[p] = src[table[row, p]]
            remote(out.at[p], dst.at[me], a2a_send.at[phase], a2a_recv.at[phase], on_chip(p)).start()
            return carry

        lax.fori_loop(1, chips, body, 0)
        dst[me] = src[table[row, me]]

    def invert():
        lane = lax.broadcasted_iota(jnp.int32, (8, 128), 1)

        def body(b, row):
            return jnp.where(lane == perm_ref[my_head, b], b, row)

        inv_row[...] = lax.fori_loop(0, chips, body, jnp.zeros((8, 128), jnp.int32))
        copy = pltpu.make_async_copy(inv_row, inv_ref, load_sem.at[8])
        copy.start()
        copy.wait()

    def all_arrived(dst, phase):
        arrived(dst.at[pl.ds(0, chips - 1)], a2a_recv.at[phase])

    def to_near(src, dst, slot, side):
        return remote(src, dst, hd_send.at[slot], hd_recv.at[slot], {"head": near[side]})

    spread(kv.at[0], in1, 0)
    wx_cross.wait_recv()
    wx_start()
    swap_own = remote(kv.at[0], kv.at[1], pair_send.at[0], pair_recv.at[0], sibling)
    swap_own.start()
    cot_swap = [to_near(cot.at[side_rows[t]], cot_m.at[t], t, t) for t in range(2)]

    cot_swap[0].start()
    wx_first()
    all_arrived(in1, 0)
    forward(in1, perm_ref, my_head, out1, kv.at[2], 1)
    cot_swap[1].start()
    wx_end_first()
    wx_second()
    invert()

    def neighbour_w(source, which):
        value = wx[source, pl.ds(which * (edge // 2), edge // 2)]
        return value.reshape(blocks * wx_rows, cols)

    for t in range(2):
        cot_swap[t].wait_recv()
        g_acc[t] = nt(cot[side_rows[t]], w[hi]) + nt(cot_m[t], w[near[t]])

    wx_wait(wx_recv, (4, 5))
    swap_wx = remote(wx.at[core], wx.at[core], pair_send.at[4], pair_recv.at[4], sibling)
    swap_wx.start()
    all_arrived(kv.at[2], 1)
    swap_partner = remote(kv.at[2], kv.at[3], pair_send.at[1], pair_recv.at[1], sibling)
    swap_partner.start()
    swap_wx.wait_recv()
    gp_swap = []
    for t in range(2):
        both = nt(cot[side_rows[t]], neighbour_w(1 - t, 0)) + nt(cot_m[t], neighbour_w(1 - t, 1))
        gp_out[t] = both.astype(BF)
        gp_swap.append(to_near(gp_out.at[t], gp_in.at[t], 2 + t, 1 - t))
        gp_swap[t].start()

    swap_own.wait_recv()
    swap_partner.wait_recv()

    def rows_of(slot, which, h):
        piece = kv[slot, pl.ds((which * heads + h) * per_head, per_head)]
        return piece.reshape(tok, width)

    def attend(h, carry):
        q_h = q[h]
        scores = [nt(rows_of(slot, 0, h), q_h) for slot in range(4)]
        top_score = functools.reduce(
            jnp.maximum, [jnp.max(s, axis=0, keepdims=True) for s in scores]
        )
        weights = [jnp.exp2((s - top_score) * (scale * math.log2(math.e))) for s in scores]
        total = functools.reduce(
            jnp.add, [jnp.sum(e, axis=0, keepdims=True) for e in weights]
        )
        inverse = 1.0 / total
        acc = None
        for slot in range(4):
            low = (weights[slot] * inverse).astype(BF)
            prob[h, slot] = low
            term = tn(rows_of(slot, 1, h), low)
            acc = term if acc is None else acc + term
        low = acc.astype(BF)
        att_t[h] = low
        att[:, pl.ds(pl.multiple_of(h * width, width), width)] = low.T
        return carry

    lax.fori_loop(0, heads, attend, 0)

    att_swap = [to_near(att.at[side_rows[t]], att_m.at[t], 4 + t, t) for t in range(2)]
    for copy in att_swap:
        copy.start()

    for t in range(2):
        gp_swap[t].wait_recv()
        both = (g_acc[t] + gp_in[t].astype(F32)).astype(BF)
        for h in range(heads):
            grad[h, side_rows[t]] = both[:, h * width:(h + 1) * width]

    def differentiate(h, slots):
        q_h = q[h]
        grad_h = grad[h]
        delta = jnp.sum(
            grad_h.T.astype(F32) * att_t[h].astype(F32), axis=0, keepdims=True
        )
        dq_t = None
        for slot in slots:
            low = prob[h, slot]
            d_prob = nt(rows_of(slot, 1, h), grad_h)
            d_score = (low.astype(F32) * ((d_prob - delta) * scale)).astype(BF)
            term = tn(rows_of(slot, 0, h), d_score)
            dq_t = term if dq_t is None else dq_t + term
            d_key = nn(d_score, q_h)
            d_value = nn(low, grad_h)
            for which, value in ((0, d_key), (1, d_value)):
                value = value.reshape(per_head, tok // per_head, width)
                where = pl.ds((which * heads + h) * per_head, per_head)
                if slot == 0:
                    own[where] = value
                else:
                    give[slot - 1, where] = value.astype(BF)
        return dq_t

    def partner_rows(h, carry):
        dq_acc[h] = differentiate(h, (3, 2))
        for which in range(2):
            where = pl.ds((which * heads + h) * per_head, per_head)
            remote(
                give.at[2, where], got.at[1, where], pair_send.at[3], pair_recv.at[3], sibling
            ).start()
        return carry

    def block_rows(h, carry):
        dq_t = dq_acc[h] + differentiate(h, (1, 0))
        dq_ref[h] = dq_t.T.astype(BF)
        return carry

    lax.fori_loop(0, heads, partner_rows, 0)
    swap_pair = remote(give.at[0], got.at[0], pair_send.at[2], pair_recv.at[2], sibling)
    arrived(got.at[1], pair_recv.at[3])
    both_cores = give[1].astype(F32) + got[1].astype(F32)
    give[1] = both_cores.astype(BF)

    spread(give.at[1], in3, 2)
    lax.fori_loop(0, heads, block_rows, 0)
    swap_pair.start()

    pp_swap = []
    for t in range(2):
        att_swap[t].wait_recv()
        both = nn(att[side_rows[t]], w[near[1 - t]]) + nn(att_m[t], neighbour_w(t, 1))
        pp_out[t] = both.astype(BF)
        pp_swap.append(to_near(pp_out.at[t], pp_in.at[t], 6 + t, 1 - t))
        pp_swap[t].start()
    for t in range(2):
        g_acc[t] = nn(att[side_rows[t]], w[hi]) + nn(att_m[t], neighbour_w(t, 0))

    all_arrived(in3, 2)
    forward(in3, inv_ref, 0, out3, back, 3)

    swap_pair.wait_recv()
    for t in range(2):
        pp_swap[t].wait_recv()
        proj_ref[side_rows[t]] = (g_acc[t] + pp_in[t].astype(F32)).astype(BF)

    all_arrived(back, 3)

    def finish(h, carry):
        for which, ref in ((0, dk_ref), (1, dv_ref)):
            where = pl.ds((which * heads + h) * per_head, per_head)
            remote_sum = (back[where].astype(F32) + got[0, where].astype(F32)).astype(BF)
            total = own[where] + remote_sum.astype(F32)
            ref[h] = total.astype(BF).reshape(tok, width)
        return carry

    lax.fori_loop(0, heads, finish, 0)

    arrived(give.at[2], pair_send.at[3])
    for phase, ref in enumerate((kv.at[0], out1, give.at[1], out3)):
        arrived(ref.at[pl.ds(0, chips - 1)], a2a_send.at[phase])
    wx_wait(wx_send, (1, 2, 3, 4, 5))
    for copy in (
        [swap_own, swap_partner, swap_pair, swap_wx, wx_cross]
        + cot_swap + gp_swap + att_swap + pp_swap
    ):
        copy.wait_send()


def hand_out(*refs):
    sources, targets, held, sem = refs[:4], refs[4:8], refs[8:12], refs[12]
    arrive = [pltpu.make_async_copy(sources[i], held[i], sem.at[i]) for i in range(4)]
    leave = [pltpu.make_async_copy(held[i], targets[i], sem.at[4 + i]) for i in range(4)]
    for copy in arrive:
        copy.start()
    for i in range(4):
        arrive[i].wait()
        leave[i].start()
    for copy in leave:
        copy.wait()


def per_device(queries, key_vectors, value_vectors, block_perm, out_weight, out_cotangent):
    chips = lax.axis_size("seq") // 2
    groups = lax.axis_size("head")
    heads, tok, width = queries.shape
    rows = 2 * heads * tok // chips
    cols = out_cotangent.shape[1]
    in_hbm = pl.BlockSpec(memory_space=pltpu.HBM)
    smem = pl.BlockSpec(memory_space=pltpu.SMEM)
    vmem = pl.BlockSpec(memory_space=pltpu.VMEM)
    mat = jax.ShapeDtypeStruct((heads, tok, width), BF)
    pieces = (chips, rows, width)
    sides = (2, tok // 2, cols)
    flat = heads * width
    edge = digits(chips)[1]
    dma = pltpu.SemaphoreType.DMA
    scratch = [
        pltpu.VMEM((8, 128), jnp.int32),
        pltpu.SMEM((8, 128), jnp.int32),
        pltpu.VMEM((4,) + pieces, BF),
        pltpu.VMEM((heads, tok, width), BF),
        pltpu.VMEM((groups, flat, cols), BF),
        pltpu.VMEM((2, edge, edge, edge, 2 * flat // chips, cols), BF),
        pltpu.VMEM((tok, cols), BF),
        pltpu.VMEM(sides, BF),
        pltpu.VMEM((2, tok // 2, flat), BF),
        pltpu.VMEM((2, tok // 2, flat), BF),
        pltpu.VMEM((2, tok // 2, max(flat, cols)), F32),
        pltpu.VMEM(pieces, BF),
        pltpu.VMEM(pieces, BF),
        pltpu.VMEM(pieces, BF),
        pltpu.VMEM(pieces, BF),
        pltpu.VMEM(pieces, BF),
        pltpu.VMEM((heads, 4, tok, tok), BF),
        pltpu.VMEM((tok, flat), BF),
        pltpu.VMEM((2, tok // 2, flat), BF),
        pltpu.VMEM((heads, width, tok), BF),
        pltpu.VMEM((heads, tok, width), BF),
        pltpu.VMEM(sides, BF),
        pltpu.VMEM(sides, BF),
        pltpu.VMEM(pieces, F32),
        pltpu.VMEM((3,) + pieces, BF),
        pltpu.VMEM((2,) + pieces, BF),
        pltpu.VMEM((heads, width, tok), F32),
        dma((9,)), dma((4,)), dma((4,)), dma((5,)), dma((5,)), dma((6,)), dma((6,)), dma((8,)), dma((8,)),
    ]
    results = pl.pallas_call(
        functools.partial(kernel, (heads, tok, width, chips, groups)),
        out_shape=(jax.ShapeDtypeStruct((tok, cols), BF), mat, mat, mat),
        in_specs=[smem] + [in_hbm] * 5,
        out_specs=(vmem,) * 4,
        scratch_shapes=scratch,
        compiler_params=pltpu.CompilerParams(
            collective_id=0, has_side_effects=True, vmem_limit_bytes=60 << 20
        ),
    )(
        block_perm,
        queries,
        key_vectors.reshape(chips // 2, rows, width),
        value_vectors.reshape(chips // 2, rows, width),
        out_weight.reshape(heads * width, -1),
        out_cotangent,
    )
    shapes = (jax.ShapeDtypeStruct((tok, cols), BF), mat, mat, mat)
    return pl.pallas_call(
        hand_out,
        out_shape=shapes,
        in_specs=[in_hbm] * 4,
        out_specs=(in_hbm,) * 4,
        scratch_shapes=[pltpu.VMEM(shape.shape, BF) for shape in shapes] + [dma((8,))],
        compiler_params=pltpu.CompilerParams(vmem_limit_bytes=60 << 20),
    )(*results)


def solution(mesh):
    return jax.shard_map(
        per_device,
        mesh=mesh,
        in_specs=(
            P("head", "seq", None),
            P("head", "seq", None),
            P("head", "seq", None),
            P("head", None),
            P("head", None, None),
            P("seq", "head"),
        ),
        out_specs=(
            P("seq", "head"),
            P("head", "seq", None),
            P("head", "seq", None),
            P("head", "seq", None),
        ),
        check_vma=False,
    )
```
